512 devices in a mesh: ctx: 32 (over y, x), head: 16 (over z, core).
Axes of the slice: x: 4, y: 8, z: 8, core: 2. Of those that a mesh axis runs over, the one named last changes fastest.
Arguments:
- activations: bfloat16 [8192, 16384], P('ctx'), may hold values from -6 to 6
- w_query: bfloat16 [16384, 2048], P('ctx', 'head'), may hold values from -0.046875 to 0.046875
- w_keyval: bfloat16 [16384, 256], P('ctx', 'head'), may hold values from -0.046875 to 0.046875
- f_query: bfloat16 [16, 128, 128], P('head'), may hold values from -1 to 1
- f_key: bfloat16 [128, 128], replicated, may hold values from -1 to 1
- w_out: bfloat16 [2048, 16384], P('ctx', 'head'), may hold values from -0.75 to 0.75
Outputs:
- sublayer_out: bfloat16 [8192, 16384], P('ctx', 'head')
The draws below stay inside these ranges and needn't reach their ends.
All inputs are finite; a program needn't handle non-finite values.
Results may differ from the reference program's by a relative error of at most 0.0086.
Values may be sent and summed in bfloat16 or wider, within the bound.
A program may use at most 64 MiB of HBM per device.

```python
import math
import jax
import jax.numpy as jnp
from jax import lax

D = 16384
HEAD_DIM = 128
GROUP = 16
WINDOW = 64
SEQ = 8192


def level_of(key, dims, split, low, high):
    level, own = 1.0, jax.random.fold_in(key, 6)
    for position, parts in split:
        steps = jnp.exp(jax.random.uniform(jax.random.fold_in(own, position), (parts,), jnp.float32, low / len(split), high / len(split)))
        level = level * jnp.repeat(steps, dims[position] // parts).reshape([-1 if axis == position else 1 for axis in range(len(dims))])
    return level


def bell_draw(rng, dims, deviation, limit, shards=(), dtype=jnp.bfloat16):
    gain = level_of(rng, dims, shards, -0.22, 0.18) if shards else 1.0
    result = jax.random.normal(rng, dims, jnp.float32) * deviation * gain
    return jnp.minimum(jnp.maximum(result, -limit), limit).astype(dtype)


def setup_inputs(seed: int = 0) -> dict:
    key_list = jax.random.split(jax.random.key(seed), 7)
    activations = bell_draw(key_list[0], (SEQ, D), 1.0, 6.0, ((0, 32),))
    w_query = bell_draw(key_list[1], (D, GROUP * HEAD_DIM), D ** -0.5, 0.046875, ((0, 32), (1, 16)))
    w_keyval = bell_draw(key_list[2], (D, 2 * HEAD_DIM), D ** -0.5, 0.046875, ((0, 32), (1, 16)))
    f_query = bell_draw(key_list[3], (GROUP, HEAD_DIM, HEAD_DIM), (HEAD_DIM // 4) ** -0.5, 1.0, ((0, 16),))
    f_key = bell_draw(key_list[4], (HEAD_DIM, HEAD_DIM), (HEAD_DIM // 4) ** -0.5, 1.0)
    w_out = bell_draw(key_list[5], (GROUP * HEAD_DIM, D), (HEAD_DIM // 2) ** -0.5, 0.75, ((0, 32), (1, 16)))
    return {"activations": activations, "w_query": w_query, "w_keyval": w_keyval, "f_query": f_query, "f_key": f_key, "w_out": w_out}


def normalized(logits):
    rising = jnp.exp(logits)
    falling = jnp.exp(-logits)
    rising = rising / lax.optimization_barrier(jnp.sum(rising, axis=-1, keepdims=True))
    falling = falling / lax.optimization_barrier(jnp.sum(falling, axis=-1, keepdims=True))
    return jnp.concatenate([rising, falling], axis=-1).astype(jnp.bfloat16)

def reference(activations, w_query, w_keyval, f_query, f_key, w_out):
    seq_rows = activations.shape[0]
    head_width = f_key.shape[0]
    heads = f_query.shape[0]
    queries = jnp.dot(activations, w_query, preferred_element_type=jnp.float32).astype(jnp.bfloat16)
    keyval = jnp.dot(activations, w_keyval, preferred_element_type=jnp.float32).astype(jnp.bfloat16)
    keys = keyval[:, :head_width]
    values = keyval[:, head_width:]
    key_feats = normalized(jnp.dot(keys, f_key, preferred_element_type=jnp.float32))
    query_heads = queries.reshape(seq_rows, heads, head_width)
    query_feats = normalized(jnp.einsum('thc,hcf->htf', query_heads.astype(jnp.float32), f_query.astype(jnp.float32)))
    scale = 1.0 / math.sqrt(head_width)
    blocks = seq_rows // WINDOW
    query_blocks = query_heads.reshape(blocks, WINDOW, heads, head_width)
    qfeat_blocks = query_feats.reshape(heads, blocks, WINDOW, 2 * head_width).transpose(1, 0, 2, 3)
    key_blocks = keys.reshape(blocks, WINDOW, head_width)
    value_blocks = values.reshape(blocks, WINDOW, head_width)
    kfeat_blocks = key_feats.reshape(blocks, WINDOW, 2 * head_width)
    offsets = jnp.arange(WINDOW)[:, None] + WINDOW - jnp.arange(2 * WINDOW)[None, :]

    def step(carry, inputs):
        matrix, totals, prev_keys, prev_vals, prev_feats = carry
        index, qblock, fblock, kblock, vblock, kfblock = inputs
        present = jnp.concatenate([jnp.full((WINDOW,), index > 0), jnp.ones((WINDOW,), bool)])
        ext_keys = jnp.concatenate([prev_keys, kblock], axis=0)
        ext_vals = jnp.concatenate([prev_vals, vblock], axis=0).astype(jnp.float32)
        ext_feats = jnp.concatenate([prev_feats, kfblock], axis=0)
        inside = (offsets >= 0) & (offsets < WINDOW) & present[None, :]
        beyond = (offsets >= WINDOW) & present[None, :]
        scores = jnp.einsum('thc,kc->htk', qblock.astype(jnp.float32), ext_keys.astype(jnp.float32)) * scale
        near_w = jnp.where(inside[None], jnp.exp(scores), 0.0)
        far_w = jnp.where(beyond[None], jnp.einsum('htf,kf->htk', fblock.astype(jnp.float32), ext_feats.astype(jnp.float32)), 0.0)
        weights = near_w + far_w
        fwide = fblock.astype(jnp.float32)
        numerator = jnp.einsum('htk,kc->htc', weights, ext_vals, precision=lax.Precision.HIGHEST)
        numerator = numerator + jnp.einsum('htf,fc->htc', fwide, matrix, precision=lax.Precision.HIGHEST)
        denominator = lax.optimization_barrier(jnp.sum(weights, axis=-1)) + jnp.einsum('htf,f->ht', fwide, totals, precision=lax.Precision.HIGHEST)
        attn_block = (numerator / denominator[..., None]).astype(jnp.bfloat16)
        keep = jnp.where(index > 0, 1.0, 0.0).astype(jnp.float32)
        matrix = matrix + keep * jnp.einsum('nf,nc->fc', prev_feats.astype(jnp.float32), prev_vals.astype(jnp.float32))
        totals = totals + keep * lax.optimization_barrier(jnp.sum(prev_feats.astype(jnp.float32), axis=0))
        return ((matrix, totals, kblock, vblock, kfblock), attn_block.transpose(1, 0, 2))
    start = (jnp.zeros((2 * head_width, head_width), jnp.float32), jnp.zeros((2 * head_width,), jnp.float32), jnp.zeros((WINDOW, head_width), jnp.bfloat16), jnp.zeros((WINDOW, head_width), jnp.bfloat16), jnp.zeros((WINDOW, 2 * head_width), jnp.bfloat16))
    inputs = (jnp.arange(blocks).astype(jnp.int32), query_blocks, qfeat_blocks, key_blocks, value_blocks, kfeat_blocks)
    final, attn_blocks = lax.scan(step, start, inputs)
    attn = attn_blocks.reshape(seq_rows, heads * head_width)
    return jnp.dot(attn, w_out, preferred_element_type=jnp.float32).astype(jnp.bfloat16)
```

```python
import math

import jax
import jax.numpy as jnp
from jax import lax
from jax.experimental import pallas as pl
from jax.experimental.pallas import tpu as pltpu
from jax.sharding import PartitionSpec as P

WINDOW = 64
NX = 4
CORES = 2
SUBS = 2
MESH = pl.DeviceIdType.MESH
F32 = jnp.float32
BF16 = jnp.bfloat16


def rem(a, b):
    return lax.rem(a, jnp.int32(b))


def div(a, b):
    return lax.div(a, jnp.int32(b))


def ring_pos(cycle, y, x, ny):
    if cycle == 0:
        return NX * y + rem(x + y, NX)
    t = rem(y + 3 * ny - 3 * x, ny)
    return 4 * (x + NX * div(t, 4)) + rem(t, 4)


def ring_node(cycle, s, ny):
    a, b = div(s, 4), rem(s, 4)
    if cycle == 0:
        y, x = a, rem(b + 4 * ny - a, NX)
    else:
        y, x = rem(3 * a + b, ny), rem(a, NX)
    return NX * y + x


def features(logits, axis):
    rising = jnp.exp(logits)
    falling = jnp.exp(-logits)
    rising = rising / jnp.sum(rising, axis=axis, keepdims=True)
    falling = falling / jnp.sum(falling, axis=axis, keepdims=True)
    return jnp.concatenate([rising, falling], axis=axis).astype(BF16)


def remote(src, dst, send_sem, recv_sem, ctx, head):
    return pltpu.make_async_remote_copy(
        src_ref=src,
        dst_ref=dst,
        send_sem=send_sem,
        recv_sem=recv_sem,
        device_id={"ctx": ctx, "head": head},
        device_id_type=MESH,
    )


def sublayer_kernel(
    nctx,
    nhead,
    x_hbm,
    wq_hbm,
    wkv_ref,
    fq_ref,
    fk_ref,
    wo_hbm,
    out_ref,
    xbuf,
    wbuf,
    mask,
    acc,
    wfull,
    kvall,
    bord,
    kfbuf,
    stx,
    sty,
    mz,
    attn,
    oacc,
    xsem,
    lsem,
    q_send,
    q_recv,
    o_send,
    o_recv,
    kv_recv,
    b_recv,
    x_recv,
    y_recv,
    m_recv,
    z_recv,
    s_recv,
    misc_send,
):
    ny, nz = nctx // NX, nhead // CORES
    hops = nctx // 2
    zhops = nz // 2
    c = lax.axis_index("ctx")
    h = lax.axis_index("head")
    y, x = div(c, NX), rem(c, NX)
    z, core = div(h, CORES), rem(h, CORES)
    tokens = x_hbm.shape[0]
    half = wq_hbm.shape[0] // 2
    ohalf = wo_hbm.shape[0] // 2
    packed = half // 8
    rows = half + packed
    dim = fk_ref.shape[0]
    width = wkv_ref.shape[1]
    sibling = CORES * z + 1 - core

    place = [ring_pos(k, y, x, ny) for k in range(2)]
    ahead = [ring_node(k, rem(place[k] + 1, nctx), ny) for k in range(2)]
    behind = [ring_node(k, rem(place[k] + nctx - 1, nctx), ny) for k in range(2)]
    target = [ahead[0], behind[0], ahead[1], behind[1]]
    limit = [hops, hops - 1, hops, hops - 1]

    def owner(stream, k):
        cycle = stream // 2
        if stream % 2 == 0:
            return ring_node(cycle, rem(place[cycle] + 2 * nctx - 1 - k, nctx), ny)
        return ring_node(cycle, rem(place[cycle] + 1 + k, nctx), ny)

    barrier = pltpu.get_barrier_semaphore()

    def greet(ctx, head):
        pl.semaphore_signal(
            barrier, inc=1, device_id={"ctx": ctx, "head": head}, device_id_type=MESH
        )

    for ctx in target:
        greet(ctx, h)
    for j in range(1, NX):
        greet(NX * y + rem(x + j, NX), h)

    @pl.loop(1, ny)
    def _(j):
        greet(NX * rem(y + j, ny) + x, h)

    @pl.loop(1, nhead)
    def _(j):
        greet(c, rem(h + j, nhead))

    following, previous = rem(c + 1, nctx), rem(c + nctx - 1, nctx)
    greet(following, h)
    greet(previous, h)

    own_q = [
        pltpu.make_async_copy(
            wq_hbm.at[pl.ds(half * k, half)],
            wbuf.at[c, k, pl.ds(0, half)],
            lsem.at[k],
        )
        for k in range(2)
    ]
    own_o = [
        pltpu.make_async_copy(
            wo_hbm.at[pl.ds(ohalf * k, ohalf)], wfull.at[c, k], lsem.at[2 + k]
        )
        for k in range(2)
    ]
    for copy in own_q:
        copy.start()

    @pl.loop(0, 2 * nctx)
    def _(j):
        pltpu.make_async_copy(
            x_hbm.at[:, pl.ds(pl.multiple_of(j * half, half), half)], xbuf.at[j], xsem
        ).start()

    for copy in own_o:
        copy.start()

    row_id = lax.broadcasted_iota(jnp.int32, (half, 8 * width), 0)
    lane_id = lax.broadcasted_iota(jnp.int32, (half, 8 * width), 1)
    group = jnp.where(div(row_id, packed) == div(lane_id, width), 1.0, 0.0)
    mask[...] = group.astype(BF16)
    spread = jnp.where(
        lax.broadcasted_iota(jnp.int32, (width, 8 * width), 0)
        == rem(lax.broadcasted_iota(jnp.int32, (width, 8 * width), 1), width),
        1.0,
        0.0,
    ).astype(BF16)
    for k in range(2):
        wide = jnp.dot(
            wkv_ref[pl.ds(half * k, half), :], spread, preferred_element_type=F32
        )
        wide = wide * group
        dense = wide[:packed]
        for j in range(1, 8):
            dense = dense + wide[packed * j : packed * (j + 1)]
        wbuf[c, k, pl.ds(half, packed)] = dense.astype(BF16)

    pl.semaphore_wait(barrier, 4 + (NX - 1) + (ny - 1) + (nhead - 1) + 2)

    piece = rows // SUBS

    def q_copy(stream, k, sub, block):
        part = wbuf.at[block, stream // 2, pl.ds(piece * sub, piece)]
        return remote(
            part, part, q_send.at[stream], q_recv.at[stream, k, sub], target[stream], h
        )

    for copy in own_q:
        copy.wait()
    for sub in range(SUBS):
        for stream in range(4):
            q_copy(stream, 0, sub, c).start()

    def product(block, k):
        part = wbuf[block, k]
        wide = jnp.concatenate([part[half:]] * 8, axis=0) * mask[...]
        weights = jnp.concatenate([part[:half], wide], axis=1)
        return jnp.dot(xbuf[2 * block + k], weights, preferred_element_type=F32)

    pltpu.make_async_copy(xbuf, xbuf, xsem).wait()
    acc[...] = product(c, 0) + product(c, 1)

    def q_step(k, receiving, sending):
        blocks = [owner(stream, k) for stream in range(4)]
        for sub in range(SUBS):
            for stream in receiving:
                q_copy(stream, k, sub, blocks[stream]).wait_recv()
                if stream in sending:
                    q_copy(stream, k + 1, sub, blocks[stream]).start()
        total = product(blocks[receiving[0]], receiving[0] // 2)
        for stream in receiving[1:]:
            total = total + product(blocks[stream], stream // 2)
        acc[...] += total

    @pl.loop(0, hops - 2)
    def _(k):
        q_step(k, (0, 1, 2, 3), (0, 1, 2, 3))

    q_step(jnp.int32(hops - 2), (0, 1, 2, 3), (0, 2))

    opiece = ohalf // SUBS

    def o_copy(stream, k, sub, block):
        part = wfull.at[block, stream // 2, pl.ds(opiece * sub, opiece)]
        return remote(
            part, part, o_send.at[stream], o_recv.at[stream, k, sub], target[stream], h
        )

    def o_step(k, receiving, sending):
        for sub in range(SUBS):
            for stream in receiving:
                block = owner(stream, k)
                o_copy(stream, k, sub, block).wait_recv()
                if stream in sending:
                    o_copy(stream, k + 1, sub, block).start()

    def o_steps(first, last):
        if first < min(last, hops - 2):

            @pl.loop(first, min(last, hops - 2))
            def _(k):
                o_step(k, (0, 1, 2, 3), (0, 1, 2, 3))

        if first <= hops - 2 < last:
            o_step(jnp.int32(hops - 2), (0, 1, 2, 3), (0, 2))
        if first <= hops - 1 < last:
            o_step(jnp.int32(hops - 1), (0, 2), ())

    for copy in own_o:
        copy.wait()
    for sub in range(SUBS):
        for stream in range(4):
            o_copy(stream, 0, sub, c).start()

    q_step(jnp.int32(hops - 1), (0, 2), ())

    queries = acc[:, :dim].astype(BF16)
    folded = acc[:, dim:].T
    own_kv = folded[:width]
    for j in range(1, 8):
        own_kv = own_kv + folded[width * j : width * (j + 1)]
    kvall[h] = own_kv.astype(BF16)

    def to_heads(buffer, sems, send):
        @pl.loop(1, nhead)
        def _(j):
            remote(
                buffer.at[h], buffer.at[h], send, sems.at[h], c, rem(h + j, nhead)
            ).start()

    def from_heads(buffer, sems, send):
        @pl.loop(1, nhead)
        def _(j):
            source = rem(h + j, nhead)
            remote(
                buffer.at[source], buffer.at[source], send, sems.at[source], c, source
            ).wait_recv()

    to_heads(kvall, kv_recv, misc_send.at[0])

    query_feats = features(
        jnp.dot(queries, fq_ref[0], preferred_element_type=F32), 1
    )
    o_steps(0, 2)

    from_heads(kvall, kv_recv, misc_send.at[0])
    edge = tokens - 2 * WINDOW
    border = remote(
        kvall.at[:, :, pl.ds(edge, 2 * WINDOW)],
        bord,
        misc_send.at[1],
        b_recv,
        following,
        h,
    )
    border.start()
    o_steps(2, 3)
    border.wait_recv()

    both = jnp.concatenate([bord[...], kvall[...]], axis=2)
    extent = tokens + 2 * WINDOW
    both = both.reshape(2 * dim, extent)
    keys, values = both[:dim], both[dim:]
    fk_t = fk_ref[...].astype(F32).T.astype(BF16)
    key_feats = features(jnp.dot(fk_t, keys, preferred_element_type=F32), 0)
    kfbuf[...] = key_feats.reshape(nhead, 2 * dim // nhead, extent)
    lowest = jnp.where(c > 0, WINDOW, 2 * WINDOW)
    mine = kfbuf[h].astype(F32)
    lane = lax.broadcasted_iota(jnp.int32, mine.shape, 1)
    mine = jnp.where((lane >= lowest) & (lane < extent - WINDOW), mine, 0.0)
    stx[x, 0] = lax.dot_general(
        mine.astype(BF16), values, (((1,), (1,)), ((), ())), preferred_element_type=F32
    )
    stx[x, 1] = jnp.broadcast_to(
        jnp.sum(mine, axis=1, keepdims=True), (mine.shape[0], dim)
    )
    for j in range(1, NX):
        remote(
            stx.at[x],
            stx.at[x],
            misc_send.at[2],
            x_recv.at[x],
            NX * y + rem(x + j, NX),
            h,
        ).start()
    o_steps(3, 5)

    for j in range(1, NX):
        source = rem(x + j, NX)
        remote(
            stx.at[source],
            stx.at[source],
            misc_send.at[2],
            x_recv.at[source],
            NX * y + source,
            h,
        ).wait_recv()
    row = stx[0] + stx[1] + stx[2] + stx[3]
    before = jnp.zeros_like(row)
    for j in range(NX - 1):
        before = before + stx[j] * jnp.where(j < x, 1.0, 0.0)
    sty[y] = row

    @pl.loop(1, ny)
    def _(j):
        remote(
            sty.at[y],
            sty.at[y],
            misc_send.at[3],
            y_recv.at[y],
            NX * rem(y + j, ny) + x,
            h,
        ).start()

    o_steps(5, 6)

    token = lax.broadcasted_iota(jnp.int32, (tokens, extent), 0)
    key_at = lax.broadcasted_iota(jnp.int32, (tokens, extent), 1)
    offset = token + 2 * WINDOW - key_at
    held = key_at >= lowest
    inside = (offset >= 0) & (offset < WINDOW) & held
    beyond = (offset >= WINDOW) & held
    scores = jnp.dot(queries, keys, preferred_element_type=F32) * (1.0 / math.sqrt(dim))
    far = jnp.dot(query_feats, key_feats, preferred_element_type=F32)
    weights = jnp.where(inside, jnp.exp(scores), 0.0) + jnp.where(beyond, far, 0.0)
    numerator = lax.dot_general(
        weights.astype(BF16),
        values,
        (((1,), (1,)), ((), ())),
        preferred_element_type=F32,
    )
    denominator = jnp.sum(weights, axis=1, keepdims=True)
    o_steps(6, 7)

    @pl.loop(1, ny)
    def _(j):
        source = rem(y + j, ny)
        remote(
            sty.at[source],
            sty.at[source],
            misc_send.at[3],
            y_recv.at[source],
            NX * source + x,
            h,
        ).wait_recv()

    for j in range(ny - 1):
        before = before + sty[j] * jnp.where(j < y, 1.0, 0.0)
    mz[h] = before.astype(BF16)
    to_heads(mz, m_recv, misc_send.at[4])
    o_steps(7, 9)
    from_heads(mz, m_recv, misc_send.at[4])
    matrix = mz[:, 0].reshape(2 * dim, dim)
    totals = mz[:, 1].reshape(2 * dim, dim)
    numerator = numerator + jnp.dot(query_feats, matrix, preferred_element_type=F32)
    denominator = denominator + jnp.dot(query_feats, totals, preferred_element_type=F32)
    attn[z, core] = (numerator / denominator).astype(BF16)

    zlimit = [zhops, zhops - 1]
    ztarget = [
        CORES * rem(z + 1, nz) + core,
        CORES * rem(z + nz - 1, nz) + core,
    ]
    tpiece = tokens // SUBS

    def z_source(stream, k):
        if stream == 0:
            return rem(z + 2 * nz - 1 - k, nz)
        return rem(z + 1 + k, nz)

    def z_copy(stream, k, sub, block):
        part = attn.at[block, core, pl.ds(tpiece * sub, tpiece)]
        return remote(
            part, part, misc_send.at[5 + stream], z_recv.at[stream, k, sub], c, ztarget[stream]
        )

    def to_sibling(block):
        remote(
            attn.at[block, core],
            attn.at[block, core],
            misc_send.at[7],
            s_recv.at[block],
            c,
            sibling,
        ).start()

    def from_sibling(block):
        remote(
            attn.at[block, 1 - core],
            attn.at[block, 1 - core],
            misc_send.at[7],
            s_recv.at[block],
            c,
            sibling,
        ).wait_recv()

    def z_step(k):
        streams = [s for s in range(2) if k < zlimit[s]]
        for sub in range(SUBS):
            for s in streams:
                block = z_source(s, k)
                z_copy(s, k, sub, block).wait_recv()
                if k + 1 < zlimit[s]:
                    z_copy(s, k + 1, sub, block).start()
        for s in streams:
            to_sibling(z_source(s, k))

    for sub in range(SUBS):
        for s in range(2):
            if zlimit[s]:
                z_copy(s, 0, sub, z).start()
    to_sibling(z)
    done = 9
    for k in range(zhops):
        upto = min(hops, done + 2) if k < zhops - 1 else hops
        o_steps(done, upto)
        done = upto
        z_step(k)

    def out_product(block):
        heads = jnp.concatenate([attn[block, 0], attn[block, 1]], axis=1)
        weights = wfull[pl.ds(2 * CORES * block, 2 * CORES)].reshape(
            CORES * dim, wo_hbm.shape[1]
        )
        return jnp.dot(heads, weights, preferred_element_type=F32)

    from_sibling(z)
    oacc[...] = out_product(z)
    for k in range(zhops):
        for s in range(2):
            if k < zlimit[s]:
                block = z_source(s, k)
                from_sibling(block)
                oacc[...] += out_product(block)
    out_ref[...] = oacc[...].astype(BF16)

    def sent(ref, sem):
        remote(ref, ref, sem, b_recv, following, h).wait_send()

    for stream in range(4):
        sent(wbuf.at[pl.ds(0, limit[stream]), 0], q_send.at[stream])
        sent(wfull.at[pl.ds(0, limit[stream]), 0], o_send.at[stream])
    sent(kvall.at[pl.ds(0, nhead - 1)], misc_send.at[0])
    sent(bord, misc_send.at[1])
    sent(stx.at[pl.ds(0, NX - 1)], misc_send.at[2])
    sent(sty.at[pl.ds(0, ny - 1)], misc_send.at[3])
    sent(mz.at[pl.ds(0, nhead - 1)], misc_send.at[4])
    for s in range(2):
        if zlimit[s]:
            sent(attn.at[pl.ds(0, zlimit[s]), 0], misc_send.at[5 + s])
    sent(attn.at[:, 0], misc_send.at[7])


def per_device(activations, w_query, w_keyval, f_query, f_key, w_out):
    nctx, nhead = lax.axis_size("ctx"), lax.axis_size("head")
    ny, nz = nctx // NX, nhead // CORES
    hops = nctx // 2
    tokens = activations.shape[0]
    half, ohalf = w_query.shape[0] // 2, w_out.shape[0] // 2
    dim, columns = f_key.shape[0], w_out.shape[1]
    width = w_keyval.shape[1]
    extent = tokens + 2 * WINDOW
    part = 2 * dim // nhead

    def kernel(*refs):
        sublayer_kernel(nctx, nhead, *refs)

    dma = pltpu.SemaphoreType.DMA
    anywhere = pl.BlockSpec(memory_space=pl.ANY)
    vmem = pl.BlockSpec(memory_space=pltpu.VMEM)
    return pl.pallas_call(
        kernel,
        out_shape=jax.ShapeDtypeStruct((tokens, columns), BF16),
        in_specs=[anywhere, anywhere, vmem, vmem, vmem, anywhere],
        out_specs=vmem,
        scratch_shapes=[
            pltpu.VMEM((2 * nctx, tokens, half), BF16),
            pltpu.VMEM((nctx, 2, half + half // 8, dim), BF16),
            pltpu.VMEM((half, 8 * width), BF16),
            pltpu.VMEM((tokens, dim + 8 * width), F32),
            pltpu.VMEM((nctx, 2, ohalf, columns), BF16),
            pltpu.VMEM((nhead, width, tokens), BF16),
            pltpu.VMEM((nhead, width, 2 * WINDOW), BF16),
            pltpu.VMEM((nhead, part, extent), BF16),
            pltpu.VMEM((NX, 2, part, dim), F32),
            pltpu.VMEM((ny, 2, part, dim), F32),
            pltpu.VMEM((nhead, 2, part, dim), BF16),
            pltpu.VMEM((nz, CORES, tokens, dim), BF16),
            pltpu.VMEM((tokens, columns), F32),
            dma,
            dma((4,)),
            dma((4,)),
            dma((4, hops, SUBS)),
            dma((4,)),
            dma((4, hops, SUBS)),
            dma((nhead,)),
            dma,
            dma((NX,)),
            dma((ny,)),
            dma((nhead,)),
            dma((2, max(nz // 2, 1), SUBS)),
            dma((nz,)),
            dma((8,)),
        ],
        compiler_params=pltpu.CompilerParams(
            collective_id=0, has_side_effects=True, vmem_limit_bytes=56 << 20
        ),
    )(activations, w_query, w_keyval, f_query, f_key, w_out)


def solution(mesh):
    in_specs = (
        P("ctx", None),
        P("ctx", "head"),
        P("ctx", "head"),
        P("head", None, None),
        P(),
        P("ctx", "head"),
    )
    out_specs = P("ctx", "head")
    return jax.shard_map(
        per_device, mesh=mesh, in_specs=in_specs, out_specs=out_specs, check_vma=False
    )
```

```python
import math

import jax
import jax.numpy as jnp
from jax import lax
from jax.experimental import pallas as pl
from jax.experimental.pallas import tpu as pltpu
from jax.sharding import PartitionSpec as P

WINDOW = 64
NX = 4
CORES = 2
MESH = pl.DeviceIdType.MESH
F32 = jnp.float32
BF16 = jnp.bfloat16


def rem(a, b):
    return lax.rem(a, jnp.int32(b))


def div(a, b):
    return lax.div(a, jnp.int32(b))


def features(logits, axis):
    rising = jnp.exp(logits)
    falling = jnp.exp(-logits)
    rising = rising / jnp.sum(rising, axis=axis, keepdims=True)
    falling = falling / jnp.sum(falling, axis=axis, keepdims=True)
    return jnp.concatenate([rising, falling], axis=axis).astype(BF16)


def remote(src, dst, send_sem, recv_sem, ctx, head):
    return pltpu.make_async_remote_copy(
        src_ref=src,
        dst_ref=dst,
        send_sem=send_sem,
        recv_sem=recv_sem,
        device_id={"ctx": ctx, "head": head},
        device_id_type=MESH,
    )


class Spread:
    def __init__(self, size, place, block, device, send_sem, recv_sem):
        self.size, self.place = size, place
        self.block, self.device = block, device
        self.send_sem, self.recv_sem = send_sem, recv_sem

    def at(self, offset):
        return rem(self.place + offset + self.size, self.size)

    def copy(self, source, offset):
        part = self.block(source)
        return remote(
            part,
            part,
            self.send_sem,
            self.recv_sem.at[source],
            *self.device(self.at(offset)),
        )

    def start(self):
        for offset in (1, -1, 2, -2):
            self.copy(self.place, offset).start()

    def wait(self, offset):
        self.copy(self.at(offset), 1).wait_recv()

    def forward_up(self):
        self.copy(self.at(-2), 1).start()
        self.copy(self.at(-2), 2).start()

    def forward_down(self):
        self.copy(self.at(2), -1).start()


class Gather:
    def __init__(self, buffer, y, x, ny, h, send, ax, ay, by, bx):
        self.buffer, self.y, self.x, self.ny, self.h = buffer, y, x, ny, h
        self.send, self.ax, self.ay, self.bx = send, ax, ay, bx
        self.b = Spread(
            ny,
            y,
            lambda source: buffer.at[NX * source + x, 1],
            lambda place: (NX * place + x, h),
            send.at[1],
            by,
        )

    def ring(self, offset):
        return rem(self.y + offset + self.ny, self.ny)

    def a_copy_x(self, source, to):
        part = self.buffer.at[NX * self.y + source, 0]
        return remote(
            part, part, self.send.at[0], self.ax.at[source], NX * self.y + to, self.h
        )

    def a_start(self):
        for j in range(1, NX):
            self.a_copy_x(self.x, rem(self.x + j, NX)).start()

    def a_wait(self):
        for j in range(1, NX):
            self.a_copy_x(rem(self.x + j, NX), self.x).wait_recv()

    def a_sets(self, k):
        last = k == self.ny // 2 - 1
        return [
            (way, col)
            for col in range(NX)
            for way in range(2)
            if not last or (way == 0) == (col < NX // 2)
        ]

    def a_source(self, way, k):
        return self.ring(-(k + 1) if way == 0 else k + 1)

    def a_copy(self, way, k, col, row):
        part = self.buffer.at[NX * row + col, 0]
        to = self.ring(1 if way == 0 else -1)
        return remote(
            part,
            part,
            self.send.at[0],
            self.ay.at[way, k, col],
            NX * to + self.x,
            self.h,
        )

    def a_first(self):
        for way, col in self.a_sets(0):
            self.a_copy(way, 0, col, self.y).start()

    def a_hop(self, k):
        onward = self.a_sets(k + 1) if k + 1 < self.ny // 2 else []
        for way, col in self.a_sets(k):
            row = self.a_source(way, k)
            self.a_copy(way, k, col, row).wait_recv()
            if (way, col) in onward:
                self.a_copy(way, k + 1, col, row).start()
        return [(self.a_source(way, k), col) for way, col in self.a_sets(k)]

    def b_copy_x(self, row, source, to):
        part = self.buffer.at[NX * row + source, 1]
        return remote(
            part, part, self.send.at[1], self.bx.at[row, source], NX * self.y + to, self.h
        )

    def b_along_x(self, offset):
        row = self.ring(offset)
        for j in range(1, NX):
            self.b_copy_x(row, self.x, rem(self.x + j, NX)).start()

    def b_near(self):
        for offset in (-1, 1):
            self.b.wait(offset)
            self.b_along_x(offset)
        self.b.wait(-2)
        self.b.forward_up()
        self.b_along_x(-2)
        self.b.wait(2)
        self.b.forward_down()
        self.b_along_x(2)

    def b_far(self):
        for offset in (-3, 3, -4):
            self.b.wait(offset)
            self.b_along_x(offset)

    def b_wait_x(self, offset):
        row = self.ring(offset)
        for j in range(1, NX):
            self.b_copy_x(row, rem(self.x + j, NX), self.x).wait_recv()
        return [(row, col) for col in range(NX)]

    def finish(self, sent):
        count = NX * self.ny - 1
        for k in range(2):
            sent(self.buffer.at[pl.ds(0, count), k], self.send.at[k])


def sublayer_kernel(
    nctx,
    nhead,
    x_hbm,
    wq_hbm,
    wkv_ref,
    fq_ref,
    fk_ref,
    wo_hbm,
    out_ref,
    xbuf,
    wbuf,
    wkv,
    acc,
    wfull,
    kvall,
    bord,
    kfbuf,
    stx,
    sty,
    mz,
    attn,
    xsem,
    lsem,
    q_send,
    q_ax,
    q_ay,
    q_by,
    q_bx,
    o_send,
    o_ax,
    o_ay,
    o_by,
    o_bx,
    w_x,
    w_y,
    kv_recv,
    b_recv,
    x_recv,
    y_recv,
    m_recv,
    z_recv,
    s_recv,
    misc_send,
):
    ny, nz = nctx // NX, nhead // CORES
    c = lax.axis_index("ctx")
    h = lax.axis_index("head")
    y, x = div(c, NX), rem(c, NX)
    z, core = div(h, CORES), rem(h, CORES)
    tokens = x_hbm.shape[0]
    half = wq_hbm.shape[0] // 2
    ohalf = wo_hbm.shape[0] // 2
    dim = fk_ref.shape[0]
    sibling = CORES * z + 1 - core
    following, previous = rem(c + 1, nctx), rem(c + nctx - 1, nctx)

    barrier = pltpu.get_barrier_semaphore()

    def greet(ctx, head):
        pl.semaphore_signal(
            barrier, inc=1, device_id={"ctx": ctx, "head": head}, device_id_type=MESH
        )

    for j in range(1, NX):
        greet(NX * y + rem(x + j, NX), h)

    @pl.loop(1, ny)
    def _(j):
        greet(NX * rem(y + j, ny) + x, h)

    @pl.loop(1, nhead)
    def _(j):
        greet(c, rem(h + j, nhead))

    greet(following, h)
    greet(previous, h)

    own_q = [
        pltpu.make_async_copy(
            wq_hbm.at[pl.ds(half * k, half)], wbuf.at[c, k], lsem.at[k]
        )
        for k in range(2)
    ]
    own_o = [
        pltpu.make_async_copy(
            wo_hbm.at[pl.ds(ohalf * k, ohalf)], wfull.at[c, k], lsem.at[2 + k]
        )
        for k in range(2)
    ]
    for copy in own_q:
        copy.start()

    @pl.loop(0, 2 * nctx)
    def _(j):
        pltpu.make_async_copy(
            x_hbm.at[:, pl.ds(pl.multiple_of(j * half, half), half)], xbuf.at[j], xsem
        ).start()

    for copy in own_o:
        copy.start()
    wkv[y, x] = wkv_ref[...]

    pl.semaphore_wait(barrier, (NX - 1) + (ny - 1) + (nhead - 1) + 2)

    q = Gather(wbuf, y, x, ny, h, q_send, q_ax, q_ay, q_by, q_bx)
    o = Gather(wfull, y, x, ny, h, o_send, o_ax, o_ay, o_by, o_bx)
    w = Spread(
        ny,
        y,
        lambda source: wkv.at[source],
        lambda place: (NX * place + x, h),
        misc_send.at[8],
        w_y,
    )

    def w_copy_x(source, to):
        part = wkv.at[y, source]
        return remote(part, part, misc_send.at[9], w_x.at[source], NX * y + to, h)

    for j in range(1, NX):
        w_copy_x(x, rem(x + j, NX)).start()
    for copy in own_q:
        copy.wait()
    q.a_start()
    q.b.start()
    for j in range(1, NX):
        w_copy_x(rem(x + j, NX), x).wait_recv()
    w.start()
    q.a_wait()
    q.a_first()
    q.b_along_x(0)

    def q_product(pairs, k):
        total = None
        for row, col in pairs:
            block = NX * row + col
            term = jnp.dot(
                xbuf[2 * block + k], wbuf[block, k], preferred_element_type=F32
            )
            total = term if total is None else total + term
        return total

    pltpu.make_async_copy(xbuf, xbuf, xsem).wait()
    acc[...] = q_product([(y, col) for col in range(NX)], 0)
    q.b_near()
    for offset in (-1, 1):
        w.wait(offset)
    w.wait(-2)
    w.forward_up()
    w.wait(2)
    w.forward_down()
    pairs0 = q.a_hop(0)
    for offset in (-3, 3, -4):
        w.wait(offset)

    contract_last = (((1,), (1,)), ((), ()))

    def kv_step(block, total):
        part = wkv[div(block, NX), rem(block, NX)]
        for k in range(2):
            total = total + lax.dot_general(
                part[:, half * k : half * (k + 1)],
                xbuf[2 * block + k],
                contract_last,
                preferred_element_type=F32,
            )
        return total

    own_kv = lax.fori_loop(
        0, nctx, kv_step, jnp.zeros((wkv.shape[2], tokens), F32), unroll=4
    )
    kvall[h] = own_kv.astype(BF16)

    def to_heads(buffer, sems, send):
        @pl.loop(1, nhead)
        def _(j):
            remote(
                buffer.at[h], buffer.at[h], send, sems.at[h], c, rem(h + j, nhead)
            ).start()

    def from_heads(buffer, sems, send):
        @pl.loop(1, nhead)
        def _(j):
            source = rem(h + j, nhead)
            remote(
                buffer.at[source], buffer.at[source], send, sems.at[source], c, source
            ).wait_recv()

    to_heads(kvall, kv_recv, misc_send.at[0])
    q.b_far()
    pairs1 = q.a_hop(1)
    acc[...] += q_product(pairs0, 0)
    acc[...] += q_product(q.b_wait_x(0), 1)

    from_heads(kvall, kv_recv, misc_send.at[0])
    border = remote(
        kvall.at[:, :, pl.ds(tokens - 2 * WINDOW, 2 * WINDOW)],
        bord,
        misc_send.at[1],
        b_recv,
        following,
        h,
    )
    border.start()
    own = kvall[...].reshape(2 * dim, tokens)
    fk_t = fk_ref[...].astype(F32).T.astype(BF16)
    own_feats = features(jnp.dot(fk_t, own[:dim], preferred_element_type=F32), 0)
    part = 2 * dim // nhead
    edge = 2 * WINDOW
    kfbuf[:, :, edge:] = own_feats.reshape(nhead, part, tokens)

    def state(feats, values):
        matrix = lax.dot_general(
            feats, values, contract_last, preferred_element_type=F32
        )
        total = jnp.sum(feats.astype(F32), axis=1, keepdims=True)
        return matrix, jnp.broadcast_to(total, (part, dim))

    matrix, total = state(kfbuf[h, :, edge:], own[dim:])
    stx[x, 0] = matrix
    stx[x, 1] = total
    for j in range(1, NX):
        remote(
            stx.at[x],
            stx.at[x],
            misc_send.at[2],
            x_recv.at[x],
            NX * y + rem(x + j, NX),
            h,
        ).start()

    pairs2 = q.a_hop(2)
    acc[...] += q_product(pairs1, 0)
    for offset in (-1, 1):
        acc[...] += q_product(q.b_wait_x(offset), 1)

    for j in range(1, NX):
        source = rem(x + j, NX)
        remote(
            stx.at[source],
            stx.at[source],
            misc_send.at[2],
            x_recv.at[source],
            NX * y + source,
            h,
        ).wait_recv()
    row = stx[0] + stx[1] + stx[2] + stx[3]
    before = jnp.zeros_like(row)
    for j in range(NX - 1):
        before = before + stx[j] * jnp.where(j < x, 1.0, 0.0)
    sty[y] = row

    @pl.loop(1, ny)
    def _(j):
        remote(
            sty.at[y],
            sty.at[y],
            misc_send.at[3],
            y_recv.at[y],
            NX * rem(y + j, ny) + x,
            h,
        ).start()

    for copy in own_o:
        copy.wait()
    o.a_start()
    o.b.start()
    acc[...] += q_product(pairs2, 0)
    for offset in (-2, 2, -3):
        acc[...] += q_product(q.b_wait_x(offset), 1)
    pairs3 = q.a_hop(3)
    o.a_wait()
    o.a_first()
    o.b_along_x(0)
    for offset in (3, -4):
        acc[...] += q_product(q.b_wait_x(offset), 1)
    acc[...] += q_product(pairs3, 0)
    queries = acc[...].astype(BF16)
    query_feats = features(jnp.dot(queries, fq_ref[0], preferred_element_type=F32), 1)
    o.b_near()

    border.wait_recv()
    edge_kv = bord[...].reshape(2 * dim, edge)
    edge_feats = features(jnp.dot(fk_t, edge_kv[:dim], preferred_element_type=F32), 0)
    kfbuf[:, :, :edge] = edge_feats.reshape(nhead, part, edge)
    lowest = jnp.where(c > 0, WINDOW, edge)
    mine = kfbuf[h, :, :edge].astype(F32)
    held = lax.broadcasted_iota(jnp.int32, mine.shape, 1) >= lowest
    matrix, total = state(jnp.where(held, mine, 0.0).astype(BF16), edge_kv[dim:])

    @pl.loop(1, ny)
    def _(j):
        source = rem(y + j, ny)
        remote(
            sty.at[source],
            sty.at[source],
            misc_send.at[3],
            y_recv.at[source],
            NX * source + x,
            h,
        ).wait_recv()

    for j in range(ny - 1):
        before = before + sty[j] * jnp.where(j < y, 1.0, 0.0)
    mz[h, 0] = (before[0] - matrix).astype(BF16)
    mz[h, 1] = (before[1] - total).astype(BF16)
    to_heads(mz, m_recv, misc_send.at[4])

    both = jnp.concatenate([bord[...], kvall[...]], axis=2)
    extent = tokens + edge
    both = both.reshape(2 * dim, extent)
    keys, values = both[:dim], both[dim:]
    key_feats = kfbuf[...].reshape(2 * dim, extent)
    token = lax.broadcasted_iota(jnp.int32, (tokens, extent), 0)
    key_at = lax.broadcasted_iota(jnp.int32, (tokens, extent), 1)
    offset = token + edge - key_at
    held = key_at >= lowest
    inside = (offset >= 0) & (offset < WINDOW) & held
    beyond = (offset >= WINDOW) & held
    scores = jnp.dot(queries, keys, preferred_element_type=F32) * (1.0 / math.sqrt(dim))
    far = jnp.dot(query_feats, key_feats, preferred_element_type=F32)
    weights = jnp.where(inside, jnp.exp(scores), 0.0) + jnp.where(beyond, far, 0.0)
    numerator = lax.dot_general(
        weights.astype(BF16), values, contract_last, preferred_element_type=F32
    )
    denominator = jnp.sum(weights, axis=1, keepdims=True)
    o.a_hop(0)
    o.b_far()

    from_heads(mz, m_recv, misc_send.at[4])
    matrix = mz[:, 0].reshape(2 * dim, dim)
    totals = mz[:, 1].reshape(2 * dim, dim)
    numerator = numerator + jnp.dot(query_feats, matrix, preferred_element_type=F32)
    denominator = denominator + jnp.dot(query_feats, totals, preferred_element_type=F32)
    attn[z, core] = (numerator / denominator).astype(BF16)

    a = Spread(
        nz,
        z,
        lambda source: attn.at[source, core],
        lambda place: (c, CORES * place + core),
        misc_send.at[5],
        z_recv,
    )

    def sibling_copy(block, side):
        part = attn.at[block, side]
        return remote(part, part, misc_send.at[6], s_recv.at[block], c, sibling)

    a.start()
    sibling_copy(z, core).start()
    o.a_hop(1)
    for offset in (-1, 1):
        a.wait(offset)
        sibling_copy(a.at(offset), core).start()
    a.wait(-2)
    a.forward_up()
    sibling_copy(a.at(-2), core).start()
    a.wait(2)
    a.forward_down()
    sibling_copy(a.at(2), core).start()
    o.a_hop(2)
    for offset in (-3, 3, -4):
        a.wait(offset)
        sibling_copy(a.at(offset), core).start()
    for offset in range(ny):
        o.b_wait_x(offset)
    o.a_hop(3)
    for offset in range(nz):
        sibling_copy(a.at(offset), 1 - core).wait_recv()

    heads = jnp.concatenate([attn[j // CORES, j % CORES] for j in range(nhead)], axis=1)
    columns = wo_hbm.shape[1]
    tile = 2 * dim

    @pl.loop(0, columns // tile)
    def _(j):
        at = pl.ds(pl.multiple_of(j * tile, tile), tile)
        weights = wfull[:, :, :, at].reshape(nhead * dim, tile)
        out_ref[:, at] = jnp.dot(heads, weights, preferred_element_type=F32).astype(
            BF16
        )

    def sent(ref, sem):
        remote(ref, ref, sem, b_recv, following, h).wait_send()

    q.finish(sent)
    o.finish(sent)
    sent(kvall.at[pl.ds(0, nhead - 1)], misc_send.at[0])
    sent(bord, misc_send.at[1])
    sent(stx.at[pl.ds(0, NX - 1)], misc_send.at[2])
    sent(sty.at[pl.ds(0, ny - 1)], misc_send.at[3])
    sent(mz.at[pl.ds(0, nhead - 1)], misc_send.at[4])
    sent(attn.at[pl.ds(0, nz - 1), 0], misc_send.at[5])
    sent(attn.at[:, 0], misc_send.at[6])
    sent(wkv.at[pl.ds(0, ny - 1)], misc_send.at[8])
    sent(wkv.at[0, pl.ds(0, NX - 1)], misc_send.at[9])


def per_device(activations, w_query, w_keyval, f_query, f_key, w_out):
    nctx, nhead = lax.axis_size("ctx"), lax.axis_size("head")
    ny, nz = nctx // NX, nhead // CORES
    tokens = activations.shape[0]
    rows, width = w_keyval.shape
    half, ohalf = rows // 2, w_out.shape[0] // 2
    dim, columns = f_key.shape[0], w_out.shape[1]
    extent = tokens + 2 * WINDOW
    part = 2 * dim // nhead

    def kernel(*refs):
        sublayer_kernel(nctx, nhead, *refs)

    dma = pltpu.SemaphoreType.DMA
    gather_sems = [
        dma((2,)),
        dma((NX,)),
        dma((2, ny // 2, NX)),
        dma((ny,)),
        dma((ny, NX)),
    ]
    anywhere = pl.BlockSpec(memory_space=pl.ANY)
    vmem = pl.BlockSpec(memory_space=pltpu.VMEM)
    return pl.pallas_call(
        kernel,
        out_shape=jax.ShapeDtypeStruct((tokens, columns), BF16),
        in_specs=[anywhere, anywhere, vmem, vmem, vmem, anywhere],
        out_specs=vmem,
        scratch_shapes=[
            pltpu.VMEM((2 * nctx, tokens, half), BF16),
            pltpu.VMEM((nctx, 2, half, dim), BF16),
            pltpu.VMEM((ny, NX, width, rows), BF16),
            pltpu.VMEM((tokens, dim), F32),
            pltpu.VMEM((nctx, 2, ohalf, columns), BF16),
            pltpu.VMEM((nhead, width, tokens), BF16),
            pltpu.VMEM((nhead, width, 2 * WINDOW), BF16),
            pltpu.VMEM((nhead, part, extent), BF16),
            pltpu.VMEM((NX, 2, part, dim), F32),
            pltpu.VMEM((ny, 2, part, dim), F32),
            pltpu.VMEM((nhead, 2, part, dim), BF16),
            pltpu.VMEM((nz, CORES, tokens, dim), BF16),
            dma,
            dma((4,)),
            *gather_sems,
            *gather_sems,
            dma((NX,)),
            dma((ny,)),
            dma((nhead,)),
            dma,
            dma((NX,)),
            dma((ny,)),
            dma((nhead,)),
            dma((nz,)),
            dma((nz,)),
            dma((10,)),
        ],
        compiler_params=pltpu.CompilerParams(
            collective_id=0, has_side_effects=True, vmem_limit_bytes=56 << 20
        ),
    )(activations, w_query, w_keyval.T, f_query, f_key, w_out)


def solution(mesh):
    in_specs = (
        P("ctx", None),
        P("ctx", "head"),
        P("ctx", "head"),
        P("head", None, None),
        P(),
        P("ctx", "head"),
    )
    out_specs = P("ctx", "head")
    return jax.shard_map(
        per_device, mesh=mesh, in_specs=in_specs, out_specs=out_specs, check_vma=False
    )
```

```python
import math

import jax
import jax.numpy as jnp
from jax import lax
from jax.experimental import pallas as pl
from jax.experimental.pallas import tpu as pltpu
from jax.sharding import PartitionSpec as P

WINDOW = 64
NX = 4
CORES = 2
MESH = pl.DeviceIdType.MESH
F32 = jnp.float32
BF16 = jnp.bfloat16


def rem(a, b):
    return lax.rem(a, jnp.int32(b))


def div(a, b):
    return lax.div(a, jnp.int32(b))


def features(logits, axis):
    rising = jnp.exp(logits)
    falling = jnp.exp(-logits)
    rising = rising / jnp.sum(rising, axis=axis, keepdims=True)
    falling = falling / jnp.sum(falling, axis=axis, keepdims=True)
    return jnp.concatenate([rising, falling], axis=axis).astype(BF16)


def remote(src, dst, send_sem, recv_sem, ctx, head):
    return pltpu.make_async_remote_copy(
        src_ref=src,
        dst_ref=dst,
        send_sem=send_sem,
        recv_sem=recv_sem,
        device_id={"ctx": ctx, "head": head},
        device_id_type=MESH,
    )


class Spread:
    def __init__(self, size, place, block, device, send_sem, recv_sem):
        self.size, self.place = size, place
        self.block, self.device = block, device
        self.send_sem, self.recv_sem = send_sem, recv_sem

    def at(self, offset):
        return rem(self.place + offset + self.size, self.size)

    def copy(self, source, offset):
        part = self.block(source)
        return remote(
            part,
            part,
            self.send_sem,
            self.recv_sem(source),
            *self.device(self.at(offset)),
        )

    def start(self):
        for offset in (1, -1, 2, -2):
            self.copy(self.place, offset).start()

    def wait(self, offset):
        self.copy(self.at(offset), 1).wait_recv()

    def forward_up(self):
        self.copy(self.at(-2), 1).start()
        self.copy(self.at(-2), 2).start()

    def forward_down(self):
        self.copy(self.at(2), -1).start()

    def near(self):
        self.wait(-2)
        self.forward_up()
        self.wait(2)
        self.forward_down()
        self.wait(-1)
        self.wait(1)

    def far(self):
        for offset in (-3, 3, -4):
            self.wait(offset)


class Ring:
    def __init__(self, size, place, block, device, send_sem, recv_sem, last):
        self.size, self.place = size, place
        self.block, self.device = block, device
        self.send_sem, self.recv_sem, self.last = send_sem, recv_sem, last

    def at(self, offset):
        return rem(self.place + offset + self.size, self.size)

    def copy(self, source, way):
        part = self.block(source)
        return remote(
            part,
            part,
            self.send_sem,
            self.recv_sem(source),
            *self.device(self.at(way)),
        )

    def ways(self, k):
        return (1, -1) if k < self.size // 2 - 1 else (self.last,)

    def start(self):
        for way in self.ways(0):
            self.copy(self.place, way).start()

    def hop(self, k):
        onward = self.ways(k + 1) if k + 1 < self.size // 2 else ()
        for way in self.ways(k):
            source = self.at(-way * (k + 1))
            self.copy(source, way).wait_recv()
            if way in onward:
                self.copy(source, way).start()


class Gather:
    def __init__(self, a, b, y, x, ny, h, send, ax, ay, by, bx):
        self.buf_a, self.buf_b = a, b
        self.y, self.x, self.ny, self.h = y, x, ny, h
        self.send, self.ax, self.bx = send, ax, bx

        def device(place):
            return NX * place + x, h

        def column(j):
            col = rem(x + j, NX)
            return Ring(
                ny,
                y,
                lambda source: a.at[NX * source + col],
                device,
                send.at[0],
                lambda source: ay.at[col, source],
                1 if j < NX // 2 else -1,
            )

        self.columns = [column(j) for j in range(NX)]
        self.b = Spread(
            ny,
            y,
            lambda source: b.at[NX * source + x],
            device,
            send.at[1],
            lambda source: by.at[source],
        )

    def row(self, offset):
        return rem(self.y + offset + self.ny, self.ny)

    def a_copy_x(self, source, to):
        part = self.buf_a.at[NX * self.y + source]
        return remote(
            part, part, self.send.at[0], self.ax.at[source], NX * self.y + to, self.h
        )

    def b_copy_x(self, row, source, to):
        part = self.buf_b.at[NX * row + source]
        return remote(
            part, part, self.send.at[1], self.bx.at[row, source], NX * self.y + to, self.h
        )

    def start(self):
        for j in range(1, NX):
            self.a_copy_x(self.x, rem(self.x + j, NX)).start()
        self.columns[0].start()
        self.b.start()
        self.b_along_x(0)

    def a_row(self):
        for j in (1, 3, 2):
            self.a_copy_x(rem(self.x + j, NX), self.x).wait_recv()
            self.columns[j].start()

    def b_along_x(self, offset):
        row = self.row(offset)
        for way in (1, NX - 1):
            self.b_copy_x(row, self.x, rem(self.x + way, NX)).start()

    def b_relay(self, *offsets):
        for offset in offsets:
            row, way = self.row(offset), 1 if offset % 2 == 0 else NX - 1
            source = rem(self.x + NX - way, NX)
            copy = self.b_copy_x(row, source, rem(self.x + way, NX))
            copy.wait_recv()
            copy.start()

    def b_near(self):
        self.b.near()
        for offset in (-1, 1, -2, 2):
            self.b_along_x(offset)

    def b_far(self):
        for offset in (-3, 3, -4):
            self.b.wait(offset)
            self.b_along_x(offset)

    def a_hop(self, k):
        for j in (1, 3, 2):
            self.columns[j].hop(k)

    def b_wait_x(self, offset):
        row, way = self.row(offset), 1 if offset % 2 == 0 else NX - 1
        for source in (rem(self.x + way, NX), rem(self.x + 2, NX)):
            self.b_copy_x(row, source, self.x).wait_recv()

    def finish(self, sent):
        count = NX * self.ny - 1
        sent(self.buf_a.at[pl.ds(0, count)], self.send.at[0])
        sent(self.buf_b.at[pl.ds(0, count)], self.send.at[1])


def sublayer_kernel(
    nctx,
    nhead,
    x_hbm,
    wq_hbm,
    wkv_ref,
    fq_ref,
    fk_ref,
    wo_hbm,
    out_ref,
    xbuf,
    wq_a,
    wq_b,
    wkv_a,
    wkv_b,
    acc,
    wo_a,
    wo_b,
    kvall,
    bord,
    kfbuf,
    stx,
    sty,
    mz,
    attn,
    xsem,
    lsem,
    q_send,
    q_ax,
    q_ay,
    q_by,
    q_bx,
    o_send,
    o_ax,
    o_ay,
    o_by,
    o_bx,
    wa_x,
    wa_y,
    wb_y,
    wb_x,
    kv_recv,
    b_recv,
    x_recv,
    y_recv,
    m_recv,
    z_recv,
    s_recv,
    misc_send,
):
    ny, nz = nctx // NX, nhead // CORES
    c = lax.axis_index("ctx")
    h = lax.axis_index("head")
    y, x = div(c, NX), rem(c, NX)
    z, core = div(h, CORES), rem(h, CORES)
    tokens = x_hbm.shape[0]
    rows = wq_hbm.shape[0]
    half = rows // 2
    low, olow = wq_a.shape[1], wo_a.shape[2]
    dim = fk_ref.shape[0]
    sibling = CORES * z + 1 - core
    following, previous = rem(c + 1, nctx), rem(c + nctx - 1, nctx)

    barrier = pltpu.get_barrier_semaphore()

    def greet(ctx, head):
        pl.semaphore_signal(
            barrier, inc=1, device_id={"ctx": ctx, "head": head}, device_id_type=MESH
        )

    for j in range(1, NX):
        greet(NX * y + rem(x + j, NX), h)

    @pl.loop(1, ny)
    def _(j):
        greet(NX * rem(y + j, ny) + x, h)

    @pl.loop(1, nhead)
    def _(j):
        greet(c, rem(h + j, nhead))

    greet(following, h)
    greet(previous, h)

    own_q = [
        pltpu.make_async_copy(wq_hbm.at[pl.ds(0, low)], wq_a.at[c], lsem.at[0]),
        pltpu.make_async_copy(
            wq_hbm.at[pl.ds(low, rows - low)], wq_b.at[c], lsem.at[1]
        ),
    ]
    own_o = [
        pltpu.make_async_copy(wo_hbm.at[:, pl.ds(0, olow)], wo_a.at[c], lsem.at[2]),
        pltpu.make_async_copy(
            wo_hbm.at[:, pl.ds(olow, wo_hbm.shape[1] - olow)], wo_b.at[c], lsem.at[3]
        ),
    ]
    for copy in own_q:
        copy.start()

    @pl.loop(0, nctx)
    def _(j):
        pltpu.make_async_copy(
            x_hbm.at[:, pl.ds(pl.multiple_of(j * rows, rows), rows)], xbuf.at[j], xsem
        ).start()

    for copy in own_o:
        copy.start()
    wkv_a[y, x] = wkv_ref[:, :half]
    wkv_b[x, y] = wkv_ref[:, half:]

    pl.semaphore_wait(barrier, (NX - 1) + (ny - 1) + (nhead - 1) + 2)

    q = Gather(wq_a, wq_b, y, x, ny, h, q_send, q_ax, q_ay, q_by, q_bx)
    o = Gather(wo_a, wo_b, y, x, ny, h, o_send, o_ax, o_ay, o_by, o_bx)

    def wa_along_x(source, to):
        part = wkv_a.at[y, source]
        return remote(part, part, misc_send.at[8], wa_x.at[source], NX * y + to, h)

    def wa_over_y(source, to):
        part = wkv_a.at[source]
        return remote(part, part, misc_send.at[9], wa_y.at[source], NX * to + x, h)

    def wb_over_y(source, to):
        part = wkv_b.at[x, source]
        return remote(part, part, misc_send.at[10], wb_y.at[source], NX * to + x, h)

    def wb_along_x(source, to):
        part = wkv_b.at[source]
        return remote(part, part, misc_send.at[11], wb_x.at[source], NX * y + to, h)

    def others(place, size, visit):
        for j in range(1, size):
            visit(rem(place + j, size))

    others(x, NX, lambda to: wa_along_x(x, to).start())
    others(y, ny, lambda to: wb_over_y(y, to).start())
    others(x, NX, lambda source: wa_along_x(source, x).wait_recv())
    others(y, ny, lambda to: wa_over_y(y, to).start())
    others(y, ny, lambda source: wb_over_y(source, y).wait_recv())
    others(x, NX, lambda to: wb_along_x(x, to).start())
    for copy in own_q:
        copy.wait()
    q.start()
    pltpu.make_async_copy(xbuf, xbuf, xsem).wait()
    others(y, ny, lambda source: wa_over_y(source, y).wait_recv())
    others(x, NX, lambda source: wb_along_x(source, x).wait_recv())

    def a_product(offset):
        first = NX * q.row(offset)
        part = jnp.concatenate(
            [xbuf[first + col, :, :low] for col in range(NX)], axis=1
        )
        weights = wq_a[pl.ds(first, NX)].reshape(NX * low, dim)
        return jnp.dot(part, weights, preferred_element_type=F32)

    def b_product(offset):
        first = NX * q.row(offset)
        total = None
        for col in range(NX):
            term = jnp.dot(
                xbuf[first + col, :, low:],
                wq_b[first + col],
                preferred_element_type=F32,
            )
            total = term if total is None else total + term
        return total

    contract_last = (((1,), (1,)), ((), ()))

    def kv_step(block, total):
        row, col = div(block, NX), rem(block, NX)
        return (
            total
            + lax.dot_general(
                wkv_a[row, col],
                xbuf[block, :, :half],
                contract_last,
                preferred_element_type=F32,
            )
            + lax.dot_general(
                wkv_b[col, row],
                xbuf[block, :, half:],
                contract_last,
                preferred_element_type=F32,
            )
        )

    own_kv = lax.fori_loop(
        0, nctx, kv_step, jnp.zeros((wkv_ref.shape[0], tokens), F32), unroll=4
    )
    kvall[h] = own_kv.astype(BF16)

    def to_heads(buffer, sems, send):
        @pl.loop(1, nhead)
        def _(j):
            remote(
                buffer.at[h], buffer.at[h], send, sems.at[h], c, rem(h + j, nhead)
            ).start()

    def from_heads(buffer, sems, send):
        @pl.loop(1, nhead)
        def _(j):
            source = rem(h + j, nhead)
            remote(
                buffer.at[source], buffer.at[source], send, sems.at[source], c, source
            ).wait_recv()

    to_heads(kvall, kv_recv, misc_send.at[0])
    q.a_row()
    q.columns[0].hop(0)
    q.b_relay(0)
    q.b_near()

    from_heads(kvall, kv_recv, misc_send.at[0])
    border = remote(
        kvall.at[:, :, pl.ds(tokens - 2 * WINDOW, 2 * WINDOW)],
        bord,
        misc_send.at[1],
        b_recv,
        following,
        h,
    )
    border.start()
    own = kvall[...].reshape(2 * dim, tokens)
    fk_t = fk_ref[...].astype(F32).T.astype(BF16)
    own_feats = features(jnp.dot(fk_t, own[:dim], preferred_element_type=F32), 0)
    part = 2 * dim // nhead
    edge = 2 * WINDOW
    kfbuf[:, :, edge:] = own_feats.reshape(nhead, part, tokens)

    def state(feats, values):
        matrix = lax.dot_general(
            feats, values, contract_last, preferred_element_type=F32
        )
        total = jnp.sum(feats.astype(F32), axis=1, keepdims=True)
        return matrix, jnp.broadcast_to(total, (part, dim))

    matrix, total = state(kfbuf[h, :, edge:], own[dim:])
    stx[x, 0] = matrix
    stx[x, 1] = total
    for j in range(1, NX):
        remote(
            stx.at[x],
            stx.at[x],
            misc_send.at[2],
            x_recv.at[x],
            NX * y + rem(x + j, NX),
            h,
        ).start()

    q.b_relay(-1, 1, -2, 2)
    q.columns[0].hop(1)
    q.b_far()
    q.a_hop(0)
    acc[...] = a_product(0)

    for j in range(1, NX):
        source = rem(x + j, NX)
        remote(
            stx.at[source],
            stx.at[source],
            misc_send.at[2],
            x_recv.at[source],
            NX * y + source,
            h,
        ).wait_recv()
    row = stx[0] + stx[1] + stx[2] + stx[3]
    before = jnp.zeros_like(row)
    for j in range(NX - 1):
        before = before + stx[j] * jnp.where(j < x, 1.0, 0.0)
    sty[y] = row

    @pl.loop(1, ny)
    def _(j):
        remote(
            sty.at[y],
            sty.at[y],
            misc_send.at[3],
            y_recv.at[y],
            NX * rem(y + j, ny) + x,
            h,
        ).start()

    q.b_relay(-3, 3, -4)
    q.columns[0].hop(2)
    q.a_hop(1)
    for copy in own_o:
        copy.wait()
    o.start()
    for offset in (-1, 1):
        acc[...] += a_product(offset)
    for offset in (0, -1, 1):
        q.b_wait_x(offset)
        acc[...] += b_product(offset)
    q.columns[0].hop(3)

    border.wait_recv()
    edge_kv = bord[...].reshape(2 * dim, edge)
    edge_feats = features(jnp.dot(fk_t, edge_kv[:dim], preferred_element_type=F32), 0)
    kfbuf[:, :, :edge] = edge_feats.reshape(nhead, part, edge)
    lowest = jnp.where(c > 0, WINDOW, edge)
    mine = kfbuf[h, :, :edge].astype(F32)
    held = lax.broadcasted_iota(jnp.int32, mine.shape, 1) >= lowest
    matrix, total = state(jnp.where(held, mine, 0.0).astype(BF16), edge_kv[dim:])

    @pl.loop(1, ny)
    def _(j):
        source = rem(y + j, ny)
        remote(
            sty.at[source],
            sty.at[source],
            misc_send.at[3],
            y_recv.at[source],
            NX * source + x,
            h,
        ).wait_recv()

    for j in range(ny - 1):
        before = before + sty[j] * jnp.where(j < y, 1.0, 0.0)
    mz[h, 0] = (before[0] - matrix).astype(BF16)
    mz[h, 1] = (before[1] - total).astype(BF16)
    to_heads(mz, m_recv, misc_send.at[4])

    q.a_hop(2)
    for offset in (-2, 2):
        acc[...] += a_product(offset)
        q.b_wait_x(offset)
        acc[...] += b_product(offset)
    o.a_row()
    o.columns[0].hop(0)
    o.b_relay(0)
    o.b_near()
    for offset in (-3, 3, -4):
        q.b_wait_x(offset)
        acc[...] += b_product(offset)
    q.a_hop(3)
    for offset in (-3, 3, -4):
        acc[...] += a_product(offset)
    queries = acc[...].astype(BF16)
    query_feats = features(jnp.dot(queries, fq_ref[0], preferred_element_type=F32), 1)

    both = jnp.concatenate([bord[...], kvall[...]], axis=2)
    extent = tokens + edge
    both = both.reshape(2 * dim, extent)
    keys, values = both[:dim], both[dim:]
    key_feats = kfbuf[...].reshape(2 * dim, extent)
    token = lax.broadcasted_iota(jnp.int32, (tokens, extent), 0)
    key_at = lax.broadcasted_iota(jnp.int32, (tokens, extent), 1)
    offset = token + edge - key_at
    held = key_at >= lowest
    inside = (offset >= 0) & (offset < WINDOW) & held
    beyond = (offset >= WINDOW) & held
    scores = jnp.dot(queries, keys, preferred_element_type=F32) * (1.0 / math.sqrt(dim))
    far = jnp.dot(query_feats, key_feats, preferred_element_type=F32)
    weights = jnp.where(inside, jnp.exp(scores), 0.0) + jnp.where(beyond, far, 0.0)
    numerator = lax.dot_general(
        weights.astype(BF16), values, contract_last, preferred_element_type=F32
    )
    denominator = jnp.sum(weights, axis=1, keepdims=True)

    from_heads(mz, m_recv, misc_send.at[4])
    matrix = mz[:, 0].reshape(2 * dim, dim)
    totals = mz[:, 1].reshape(2 * dim, dim)
    numerator = numerator + jnp.dot(query_feats, matrix, preferred_element_type=F32)
    denominator = denominator + jnp.dot(query_feats, totals, preferred_element_type=F32)
    attn[z, core] = (numerator / denominator).astype(BF16)

    a = Spread(
        nz,
        z,
        lambda source: attn.at[source, core],
        lambda place: (c, CORES * place + core),
        misc_send.at[5],
        lambda source: z_recv.at[source],
    )

    def sibling_copy(block, side):
        part = attn.at[block, side]
        return remote(part, part, misc_send.at[6], s_recv.at[block], c, sibling)

    a.start()
    sibling_copy(z, core).start()
    o.a_hop(0)
    o.columns[0].hop(1)
    o.b_relay(-1, 1, -2, 2)
    o.b_far()
    a.wait(-2)
    a.forward_up()
    sibling_copy(a.at(-2), core).start()
    a.wait(2)
    a.forward_down()
    sibling_copy(a.at(2), core).start()
    o.a_hop(1)
    o.columns[0].hop(2)
    o.b_relay(-3, 3, -4)
    for offset in (-1, 1, -3, 3, -4):
        a.wait(offset)
        sibling_copy(a.at(offset), core).start()
    o.a_hop(2)
    o.columns[0].hop(3)
    for offset in range(ny):
        o.b_wait_x(offset)
    o.a_hop(3)
    for offset in range(nz):
        sibling_copy(a.at(offset), 1 - core).wait_recv()

    heads = jnp.concatenate([attn[j // CORES, j % CORES] for j in range(nhead)], axis=1)
    start = 0
    for weights in (wo_a, wo_b):
        for at in range(0, weights.shape[2], 2 * dim):
            size = min(2 * dim, weights.shape[2] - at)
            tile = weights[:, :, at : at + size].reshape(nhead * dim, size)
            out_ref[:, start : start + size] = jnp.dot(
                heads, tile, preferred_element_type=F32
            ).astype(BF16)
            start += size

    def sent(ref, sem):
        remote(ref, ref, sem, b_recv, following, h).wait_send()

    q.finish(sent)
    o.finish(sent)
    sent(kvall.at[pl.ds(0, nhead - 1)], misc_send.at[0])
    sent(bord, misc_send.at[1])
    sent(stx.at[pl.ds(0, NX - 1)], misc_send.at[2])
    sent(sty.at[pl.ds(0, ny - 1)], misc_send.at[3])
    sent(mz.at[pl.ds(0, nhead - 1)], misc_send.at[4])
    sent(attn.at[pl.ds(0, nz - 1), 0], misc_send.at[5])
    sent(attn.at[:, 0], misc_send.at[6])
    sent(wkv_a.at[0, pl.ds(0, NX - 1)], misc_send.at[8])
    sent(wkv_a.at[pl.ds(0, ny - 1)], misc_send.at[9])
    sent(wkv_b.at[0, pl.ds(0, ny - 1)], misc_send.at[10])
    sent(wkv_b.at[pl.ds(0, NX - 1)], misc_send.at[11])


def per_device(activations, w_query, w_keyval, f_query, f_key, w_out):
    nctx, nhead = lax.axis_size("ctx"), lax.axis_size("head")
    ny, nz = nctx // NX, nhead // CORES
    tokens = activations.shape[0]
    rows, width = w_keyval.shape
    low, orows = rows // 2, w_out.shape[0]
    dim, columns = f_key.shape[0], w_out.shape[1]
    olow = columns // 2
    extent = tokens + 2 * WINDOW
    part = 2 * dim // nhead

    def kernel(*refs):
        sublayer_kernel(nctx, nhead, *refs)

    dma = pltpu.SemaphoreType.DMA
    gather_sems = [
        dma((2,)),
        dma((NX,)),
        dma((NX, ny)),
        dma((ny,)),
        dma((ny, NX)),
    ]
    anywhere = pl.BlockSpec(memory_space=pl.ANY)
    vmem = pl.BlockSpec(memory_space=pltpu.VMEM)
    return pl.pallas_call(
        kernel,
        out_shape=jax.ShapeDtypeStruct((tokens, columns), BF16),
        in_specs=[anywhere, anywhere, vmem, vmem, vmem, anywhere],
        out_specs=vmem,
        scratch_shapes=[
            pltpu.VMEM((nctx, tokens, rows), BF16),
            pltpu.VMEM((nctx, low, dim), BF16),
            pltpu.VMEM((nctx, rows - low, dim), BF16),
            pltpu.VMEM((ny, NX, width, rows // 2), BF16),
            pltpu.VMEM((NX, ny, width, rows // 2), BF16),
            pltpu.VMEM((tokens, dim), F32),
            pltpu.VMEM((nctx, orows, olow), BF16),
            pltpu.VMEM((nctx, orows, columns - olow), BF16),
            pltpu.VMEM((nhead, width, tokens), BF16),
            pltpu.VMEM((nhead, width, 2 * WINDOW), BF16),
            pltpu.VMEM((nhead, part, extent), BF16),
            pltpu.VMEM((NX, 2, part, dim), F32),
            pltpu.VMEM((ny, 2, part, dim), F32),
            pltpu.VMEM((nhead, 2, part, dim), BF16),
            pltpu.VMEM((nz, CORES, tokens, dim), BF16),
            dma,
            dma((4,)),
            *gather_sems,
            *gather_sems,
            dma((NX,)),
            dma((ny,)),
            dma((ny,)),
            dma((NX,)),
            dma((nhead,)),
            dma,
            dma((NX,)),
            dma((ny,)),
            dma((nhead,)),
            dma((nz,)),
            dma((nz,)),
            dma((12,)),
        ],
        compiler_params=pltpu.CompilerParams(
            collective_id=0, has_side_effects=True, vmem_limit_bytes=56 << 20
        ),
    )(activations, w_query, w_keyval.T, f_query, f_key, w_out)


def solution(mesh):
    in_specs = (
        P("ctx", None),
        P("ctx", "head"),
        P("ctx", "head"),
        P("head", None, None),
        P(),
        P("ctx", "head"),
    )
    out_specs = P("ctx", "head")
    return jax.shard_map(
        per_device, mesh=mesh, in_specs=in_specs, out_specs=out_specs, check_vma=False
    )
```

```python
import math

import jax
import jax.numpy as jnp
from jax import lax
from jax.experimental import pallas as pl
from jax.experimental.pallas import tpu as pltpu
from jax.sharding import PartitionSpec as P

WINDOW = 64
NX = 4
CORES = 2
MESH = pl.DeviceIdType.MESH
F32 = jnp.float32
BF16 = jnp.bfloat16


def rem(a, b):
    return lax.rem(a, jnp.int32(b))


def div(a, b):
    return lax.div(a, jnp.int32(b))


def features(logits, axis):
    rising = jnp.exp(logits)
    falling = jnp.exp(-logits)
    rising = rising / jnp.sum(rising, axis=axis, keepdims=True)
    falling = falling / jnp.sum(falling, axis=axis, keepdims=True)
    return jnp.concatenate([rising, falling], axis=axis).astype(BF16)


def remote(src, dst, send_sem, recv_sem, ctx, head):
    return pltpu.make_async_remote_copy(
        src_ref=src,
        dst_ref=dst,
        send_sem=send_sem,
        recv_sem=recv_sem,
        device_id={"ctx": ctx, "head": head},
        device_id_type=MESH,
    )


class Spread:
    def __init__(self, size, place, block, device, send_sem, recv_sem):
        self.size, self.place = size, place
        self.block, self.device = block, device
        self.send_sem, self.recv_sem = send_sem, recv_sem

    def at(self, offset):
        return rem(self.place + offset + self.size, self.size)

    def copy(self, source, offset):
        part = self.block(source)
        return remote(
            part,
            part,
            self.send_sem,
            self.recv_sem(source),
            *self.device(self.at(offset)),
        )

    def start(self):
        for offset in (1, -1, 2, -2):
            self.copy(self.place, offset).start()

    def wait(self, offset):
        self.copy(self.at(offset), 1).wait_recv()

    def forward_up(self):
        self.copy(self.at(-2), 1).start()
        self.copy(self.at(-2), 2).start()

    def forward_down(self):
        self.copy(self.at(2), -1).start()

    def near(self):
        self.wait(-2)
        self.forward_up()
        self.wait(2)
        self.forward_down()
        self.wait(-1)
        self.wait(1)

    def far(self):
        for offset in (-3, 3, -4):
            self.wait(offset)


class Ring:
    def __init__(self, size, place, block, device, send_sem, recv_sem, last):
        self.size, self.place = size, place
        self.block, self.device = block, device
        self.send_sem, self.recv_sem, self.last = send_sem, recv_sem, last

    def at(self, offset):
        return rem(self.place + offset + self.size, self.size)

    def copy(self, source, way):
        part = self.block(source)
        return remote(
            part,
            part,
            self.send_sem,
            self.recv_sem(source),
            *self.device(self.at(way)),
        )

    def ways(self, k):
        return (1, -1) if k < self.size // 2 - 1 else (self.last,)

    def start(self):
        for way in self.ways(0):
            self.copy(self.place, way).start()

    def hop(self, k):
        onward = self.ways(k + 1) if k + 1 < self.size // 2 else ()
        for way in self.ways(k):
            source = self.at(-way * (k + 1))
            self.copy(source, way).wait_recv()
            if way in onward:
                self.copy(source, way).start()


class Gather:
    def __init__(self, a, b, y, x, ny, h, send, ax, ay, by, bx):
        self.buf_a, self.buf_b = a, b
        self.y, self.x, self.ny, self.h = y, x, ny, h
        self.send, self.ax, self.bx = send, ax, bx

        def device(place):
            return NX * place + x, h

        def column(j):
            col = rem(x + j, NX)
            return Ring(
                ny,
                y,
                lambda source: a.at[NX * source + col],
                device,
                send.at[0],
                lambda source: ay.at[col, source],
                1 if j < NX // 2 else -1,
            )

        self.columns = [column(j) for j in range(NX)]
        self.b = Spread(
            ny,
            y,
            lambda source: b.at[NX * source + x],
            device,
            send.at[1],
            lambda source: by.at[source],
        )

    def row(self, offset):
        return rem(self.y + offset + self.ny, self.ny)

    def a_copy_x(self, source, to):
        part = self.buf_a.at[NX * self.y + source]
        return remote(
            part, part, self.send.at[0], self.ax.at[source], NX * self.y + to, self.h
        )

    def b_copy_x(self, row, source, to):
        part = self.buf_b.at[NX * row + source]
        return remote(
            part, part, self.send.at[1], self.bx.at[row, source], NX * self.y + to, self.h
        )

    def start(self):
        for j in range(1, NX):
            self.a_copy_x(self.x, rem(self.x + j, NX)).start()
        self.columns[0].start()
        self.b.start()
        self.b_along_x(0)

    def a_row(self):
        for j in (1, 3, 2):
            self.a_copy_x(rem(self.x + j, NX), self.x).wait_recv()
            self.columns[j].start()

    def b_along_x(self, offset):
        row = self.row(offset)
        for way in (1, NX - 1):
            self.b_copy_x(row, self.x, rem(self.x + way, NX)).start()

    def b_relay(self, *offsets):
        for offset in offsets:
            row, way = self.row(offset), 1 if offset % 2 == 0 else NX - 1
            source = rem(self.x + NX - way, NX)
            copy = self.b_copy_x(row, source, rem(self.x + way, NX))
            copy.wait_recv()
            copy.start()

    def b_near(self):
        self.b.near()
        for offset in (-1, 1, -2, 2):
            self.b_along_x(offset)

    def b_far(self):
        for offset in (-3, 3, -4):
            self.b.wait(offset)
            self.b_along_x(offset)

    def a_hop(self, k):
        for j in (1, 3, 2):
            self.columns[j].hop(k)

    def b_wait_x(self, offset):
        row, way = self.row(offset), 1 if offset % 2 == 0 else NX - 1
        for source in (rem(self.x + way, NX), rem(self.x + 2, NX)):
            self.b_copy_x(row, source, self.x).wait_recv()

    def finish(self, sent):
        count = NX * self.ny - 1
        sent(self.buf_a.at[pl.ds(0, count)], self.send.at[0])
        sent(self.buf_b.at[pl.ds(0, count)], self.send.at[1])


def sublayer_kernel(
    nctx,
    nhead,
    x_hbm,
    wq_hbm,
    wkv_ref,
    fq_ref,
    fk_ref,
    wo_hbm,
    out_ref,
    xbuf,
    wq_a,
    wq_b,
    wkv_a,
    wkv_b,
    acc,
    wo_a,
    wo_b,
    kvall,
    bord,
    kfbuf,
    stx,
    sty,
    mz,
    attn,
    xsem,
    lsem,
    q_send,
    q_ax,
    q_ay,
    q_by,
    q_bx,
    o_send,
    o_ax,
    o_ay,
    o_by,
    o_bx,
    wa_x,
    wa_y,
    wb_y,
    wb_x,
    kv_recv,
    b_recv,
    x_recv,
    y_recv,
    m_recv,
    z_recv,
    s_recv,
    misc_send,
):
    ny, nz = nctx // NX, nhead // CORES
    c = lax.axis_index("ctx")
    h = lax.axis_index("head")
    y, x = div(c, NX), rem(c, NX)
    z, core = div(h, CORES), rem(h, CORES)
    tokens = x_hbm.shape[0]
    rows = wq_hbm.shape[0]
    half = rows // 2
    low, olow = wq_a.shape[1], wo_a.shape[2]
    dim = fk_ref.shape[0]
    sibling = CORES * z + 1 - core
    following, previous = rem(c + 1, nctx), rem(c + nctx - 1, nctx)

    barrier = pltpu.get_barrier_semaphore()

    def greet(ctx, head):
        pl.semaphore_signal(
            barrier, inc=1, device_id={"ctx": ctx, "head": head}, device_id_type=MESH
        )

    for j in range(1, NX):
        greet(NX * y + rem(x + j, NX), h)

    @pl.loop(1, ny)
    def _(j):
        greet(NX * rem(y + j, ny) + x, h)

    @pl.loop(1, nhead)
    def _(j):
        greet(c, rem(h + j, nhead))

    greet(following, h)
    greet(previous, h)

    own_q = [
        pltpu.make_async_copy(wq_hbm.at[pl.ds(0, low)], wq_a.at[c], lsem.at[0]),
        pltpu.make_async_copy(
            wq_hbm.at[pl.ds(low, rows - low)], wq_b.at[c], lsem.at[1]
        ),
    ]
    own_o = [
        pltpu.make_async_copy(wo_hbm.at[:, pl.ds(0, olow)], wo_a.at[c], lsem.at[2]),
        pltpu.make_async_copy(
            wo_hbm.at[:, pl.ds(olow, wo_hbm.shape[1] - olow)], wo_b.at[c], lsem.at[3]
        ),
    ]
    for copy in own_q:
        copy.start()

    @pl.loop(0, nctx)
    def _(j):
        pltpu.make_async_copy(
            x_hbm.at[:, pl.ds(pl.multiple_of(j * rows, rows), rows)], xbuf.at[j], xsem
        ).start()

    for copy in own_o:
        copy.start()
    wkv_a[y, x] = wkv_ref[:, :half]
    wkv_b[x, y] = wkv_ref[:, half:]

    pl.semaphore_wait(barrier, (NX - 1) + (ny - 1) + (nhead - 1) + 2)

    q = Gather(wq_a, wq_b, y, x, ny, h, q_send, q_ax, q_ay, q_by, q_bx)
    o = Gather(wo_a, wo_b, y, x, ny, h, o_send, o_ax, o_ay, o_by, o_bx)

    def wa_along_x(source, to):
        part = wkv_a.at[y, source]
        return remote(part, part, misc_send.at[8], wa_x.at[source], NX * y + to, h)

    def wa_over_y(source, to):
        part = wkv_a.at[source]
        return remote(part, part, misc_send.at[9], wa_y.at[source], NX * to + x, h)

    def wb_over_y(source, to):
        part = wkv_b.at[x, source]
        return remote(part, part, misc_send.at[10], wb_y.at[source], NX * to + x, h)

    def wb_along_x(source, to):
        part = wkv_b.at[source]
        return remote(part, part, misc_send.at[11], wb_x.at[source], NX * y + to, h)

    def others(place, size, visit):
        for j in range(1, size):
            visit(rem(place + j, size))

    others(x, NX, lambda to: wa_along_x(x, to).start())
    others(y, ny, lambda to: wb_over_y(y, to).start())
    others(x, NX, lambda source: wa_along_x(source, x).wait_recv())
    others(y, ny, lambda to: wa_over_y(y, to).start())
    others(y, ny, lambda source: wb_over_y(source, y).wait_recv())
    others(x, NX, lambda to: wb_along_x(x, to).start())
    for copy in own_q:
        copy.wait()
    q.start()
    pltpu.make_async_copy(xbuf, xbuf, xsem).wait()
    others(y, ny, lambda source: wa_over_y(source, y).wait_recv())
    others(x, NX, lambda source: wb_along_x(source, x).wait_recv())

    def a_product(offset):
        first = NX * q.row(offset)
        part = jnp.concatenate(
            [xbuf[first + col, :, :low] for col in range(NX)], axis=1
        )
        weights = wq_a[pl.ds(first, NX)].reshape(NX * low, dim)
        return jnp.dot(part, weights, preferred_element_type=F32)

    def b_product(offset):
        first = NX * q.row(offset)
        total = None
        for col in range(NX):
            term = jnp.dot(
                xbuf[first + col, :, low:],
                wq_b[first + col],
                preferred_element_type=F32,
            )
            total = term if total is None else total + term
        return total

    contract_last = (((1,), (1,)), ((), ()))

    def kv_step(block, total):
        row, col = div(block, NX), rem(block, NX)
        return (
            total
            + lax.dot_general(
                wkv_a[row, col],
                xbuf[block, :, :half],
                contract_last,
                preferred_element_type=F32,
            )
            + lax.dot_general(
                wkv_b[col, row],
                xbuf[block, :, half:],
                contract_last,
                preferred_element_type=F32,
            )
        )

    own_kv = lax.fori_loop(
        0, nctx, kv_step, jnp.zeros((wkv_ref.shape[0], tokens), F32), unroll=4
    )
    kvall[h] = own_kv.astype(BF16)

    def to_heads(buffer, sems, send):
        @pl.loop(1, nhead)
        def _(j):
            remote(
                buffer.at[h], buffer.at[h], send, sems.at[h], c, rem(h + j, nhead)
            ).start()

    def from_heads(buffer, sems, send):
        @pl.loop(1, nhead)
        def _(j):
            source = rem(h + j, nhead)
            remote(
                buffer.at[source], buffer.at[source], send, sems.at[source], c, source
            ).wait_recv()

    to_heads(kvall, kv_recv, misc_send.at[0])
    q.a_row()
    q.columns[0].hop(0)
    q.b_relay(0)
    q.b_near()

    from_heads(kvall, kv_recv, misc_send.at[0])
    border = remote(
        kvall.at[:, :, pl.ds(tokens - 2 * WINDOW, 2 * WINDOW)],
        bord,
        misc_send.at[1],
        b_recv,
        following,
        h,
    )
    border.start()
    own = kvall[...].reshape(2 * dim, tokens)
    fk_t = fk_ref[...].astype(F32).T.astype(BF16)
    own_feats = features(jnp.dot(fk_t, own[:dim], preferred_element_type=F32), 0)
    part = 2 * dim // nhead
    edge = 2 * WINDOW
    kfbuf[:, :, edge:] = own_feats.reshape(nhead, part, tokens)

    def state(feats, values):
        matrix = lax.dot_general(
            feats, values, contract_last, preferred_element_type=F32
        )
        total = jnp.sum(feats.astype(F32), axis=1, keepdims=True)
        return matrix, jnp.broadcast_to(total, (part, dim))

    matrix, total = state(kfbuf[h, :, edge:], own[dim:])
    stx[x, 0] = matrix
    stx[x, 1] = total
    for j in range(1, NX):
        remote(
            stx.at[x],
            stx.at[x],
            misc_send.at[2],
            x_recv.at[x],
            NX * y + rem(x + j, NX),
            h,
        ).start()

    q.b_relay(-1, 1, -2, 2)
    q.columns[0].hop(1)
    q.b_far()
    q.a_hop(0)
    acc[...] = a_product(0)

    for j in range(1, NX):
        source = rem(x + j, NX)
        remote(
            stx.at[source],
            stx.at[source],
            misc_send.at[2],
            x_recv.at[source],
            NX * y + source,
            h,
        ).wait_recv()
    row = stx[0] + stx[1] + stx[2] + stx[3]
    before = jnp.zeros_like(row)
    for j in range(NX - 1):
        before = before + stx[j] * jnp.where(j < x, 1.0, 0.0)
    sty[y] = row

    @pl.loop(1, ny)
    def _(j):
        remote(
            sty.at[y],
            sty.at[y],
            misc_send.at[3],
            y_recv.at[y],
            NX * rem(y + j, ny) + x,
            h,
        ).start()

    q.b_relay(-3, 3, -4)
    q.columns[0].hop(2)
    q.a_hop(1)
    for copy in own_o:
        copy.wait()
    o.start()
    for offset in (-1, 1):
        acc[...] += a_product(offset)
    for offset in (0, -1, 1):
        q.b_wait_x(offset)
        acc[...] += b_product(offset)
    q.columns[0].hop(3)

    border.wait_recv()
    edge_kv = bord[...].reshape(2 * dim, edge)
    edge_feats = features(jnp.dot(fk_t, edge_kv[:dim], preferred_element_type=F32), 0)
    kfbuf[:, :, :edge] = edge_feats.reshape(nhead, part, edge)
    lowest = jnp.where(c > 0, WINDOW, edge)
    mine = kfbuf[h, :, :edge].astype(F32)
    held = lax.broadcasted_iota(jnp.int32, mine.shape, 1) >= lowest
    matrix, total = state(jnp.where(held, mine, 0.0).astype(BF16), edge_kv[dim:])

    @pl.loop(1, ny)
    def _(j):
        source = rem(y + j, ny)
        remote(
            sty.at[source],
            sty.at[source],
            misc_send.at[3],
            y_recv.at[source],
            NX * source + x,
            h,
        ).wait_recv()

    for j in range(ny - 1):
        before = before + sty[j] * jnp.where(j < y, 1.0, 0.0)
    mz[h, 0] = (before[0] - matrix).astype(BF16)
    mz[h, 1] = (before[1] - total).astype(BF16)
    to_heads(mz, m_recv, misc_send.at[4])

    q.a_hop(2)
    for offset in (-2, 2):
        acc[...] += a_product(offset)
        q.b_wait_x(offset)
        acc[...] += b_product(offset)
    o.a_row()
    o.columns[0].hop(0)
    o.b_relay(0)
    o.b_near()
    for offset in (-3, 3, -4):
        q.b_wait_x(offset)
        acc[...] += b_product(offset)
    q.a_hop(3)
    for offset in (-3, 3, -4):
        acc[...] += a_product(offset)
    queries = acc[...].astype(BF16)
    query_feats = features(jnp.dot(queries, fq_ref[0], preferred_element_type=F32), 1)

    both = jnp.concatenate([bord[...], kvall[...]], axis=2)
    extent = tokens + edge
    both = both.reshape(2 * dim, extent)
    keys, values = both[:dim], both[dim:]
    key_feats = kfbuf[...].reshape(2 * dim, extent)
    token = lax.broadcasted_iota(jnp.int32, (tokens, extent), 0)
    key_at = lax.broadcasted_iota(jnp.int32, (tokens, extent), 1)
    offset = token + edge - key_at
    held = key_at >= lowest
    inside = (offset >= 0) & (offset < WINDOW) & held
    beyond = (offset >= WINDOW) & held
    scores = jnp.dot(queries, keys, preferred_element_type=F32) * (1.0 / math.sqrt(dim))
    far = jnp.dot(query_feats, key_feats, preferred_element_type=F32)
    weights = jnp.where(inside, jnp.exp(scores), 0.0) + jnp.where(beyond, far, 0.0)
    numerator = lax.dot_general(
        weights.astype(BF16), values, contract_last, preferred_element_type=F32
    )
    denominator = jnp.sum(weights, axis=1, keepdims=True)

    from_heads(mz, m_recv, misc_send.at[4])
    matrix = mz[:, 0].reshape(2 * dim, dim)
    totals = mz[:, 1].reshape(2 * dim, dim)
    numerator = numerator + jnp.dot(query_feats, matrix, preferred_element_type=F32)
    denominator = denominator + jnp.dot(query_feats, totals, preferred_element_type=F32)
    attn[z, core] = (numerator / denominator).astype(BF16)

    a = Spread(
        nz,
        z,
        lambda source: attn.at[source, core],
        lambda place: (c, CORES * place + core),
        misc_send.at[5],
        lambda source: z_recv.at[source],
    )

    def sibling_copy(block, side):
        part = attn.at[block, side]
        return remote(part, part, misc_send.at[6], s_recv.at[block], c, sibling)

    a.start()
    sibling_copy(z, core).start()
    o.a_hop(0)
    o.columns[0].hop(1)
    o.b_relay(-1, 1, -2, 2)
    o.b_far()
    a.wait(-2)
    a.forward_up()
    sibling_copy(a.at(-2), core).start()
    a.wait(2)
    a.forward_down()
    sibling_copy(a.at(2), core).start()
    o.a_hop(1)
    o.columns[0].hop(2)
    o.b_relay(-3, 3, -4)
    for offset in (-1, 1, -3, 3, -4):
        a.wait(offset)
        sibling_copy(a.at(offset), core).start()
    o.a_hop(2)
    o.columns[0].hop(3)
    for offset in range(ny):
        o.b_wait_x(offset)
    o.a_hop(3)
    for offset in range(nz):
        sibling_copy(a.at(offset), 1 - core).wait_recv()

    heads = jnp.concatenate([attn[j // CORES, j % CORES] for j in range(nhead)], axis=1)
    start = 0
    for weights in (wo_a, wo_b):
        for at in range(0, weights.shape[2], 2 * dim):
            size = min(2 * dim, weights.shape[2] - at)
            tile = weights[:, :, at : at + size].reshape(nhead * dim, size)
            out_ref[:, start : start + size] = jnp.dot(
                heads, tile, preferred_element_type=F32
            ).astype(BF16)
            start += size

    def sent(ref, sem):
        remote(ref, ref, sem, b_recv, following, h).wait_send()

    q.finish(sent)
    o.finish(sent)
    sent(kvall.at[pl.ds(0, nhead - 1)], misc_send.at[0])
    sent(bord, misc_send.at[1])
    sent(stx.at[pl.ds(0, NX - 1)], misc_send.at[2])
    sent(sty.at[pl.ds(0, ny - 1)], misc_send.at[3])
    sent(mz.at[pl.ds(0, nhead - 1)], misc_send.at[4])
    sent(attn.at[pl.ds(0, nz - 1), 0], misc_send.at[5])
    sent(attn.at[:, 0], misc_send.at[6])
    sent(wkv_a.at[0, pl.ds(0, NX - 1)], misc_send.at[8])
    sent(wkv_a.at[pl.ds(0, ny - 1)], misc_send.at[9])
    sent(wkv_b.at[0, pl.ds(0, ny - 1)], misc_send.at[10])
    sent(wkv_b.at[pl.ds(0, NX - 1)], misc_send.at[11])


def per_device(activations, w_query, w_keyval, f_query, f_key, w_out):
    nctx, nhead = lax.axis_size("ctx"), lax.axis_size("head")
    ny, nz = nctx // NX, nhead // CORES
    tokens = activations.shape[0]
    rows, width = w_keyval.shape
    low, orows = rows // 2, w_out.shape[0]
    dim, columns = f_key.shape[0], w_out.shape[1]
    olow = 3 * columns // 8
    extent = tokens + 2 * WINDOW
    part = 2 * dim // nhead

    def kernel(*refs):
        sublayer_kernel(nctx, nhead, *refs)

    dma = pltpu.SemaphoreType.DMA
    gather_sems = [
        dma((2,)),
        dma((NX,)),
        dma((NX, ny)),
        dma((ny,)),
        dma((ny, NX)),
    ]
    anywhere = pl.BlockSpec(memory_space=pl.ANY)
    vmem = pl.BlockSpec(memory_space=pltpu.VMEM)
    return pl.pallas_call(
        kernel,
        out_shape=jax.ShapeDtypeStruct((tokens, columns), BF16),
        in_specs=[anywhere, anywhere, vmem, vmem, vmem, anywhere],
        out_specs=vmem,
        scratch_shapes=[
            pltpu.VMEM((nctx, tokens, rows), BF16),
            pltpu.VMEM((nctx, low, dim), BF16),
            pltpu.VMEM((nctx, rows - low, dim), BF16),
            pltpu.VMEM((ny, NX, width, rows // 2), BF16),
            pltpu.VMEM((NX, ny, width, rows // 2), BF16),
            pltpu.VMEM((tokens, dim), F32),
            pltpu.VMEM((nctx, orows, olow), BF16),
            pltpu.VMEM((nctx, orows, columns - olow), BF16),
            pltpu.VMEM((nhead, width, tokens), BF16),
            pltpu.VMEM((nhead, width, 2 * WINDOW), BF16),
            pltpu.VMEM((nhead, part, extent), BF16),
            pltpu.VMEM((NX, 2, part, dim), F32),
            pltpu.VMEM((ny, 2, part, dim), F32),
            pltpu.VMEM((nhead, 2, part, dim), BF16),
            pltpu.VMEM((nz, CORES, tokens, dim), BF16),
            dma,
            dma((4,)),
            *gather_sems,
            *gather_sems,
            dma((NX,)),
            dma((ny,)),
            dma((ny,)),
            dma((NX,)),
            dma((nhead,)),
            dma,
            dma((NX,)),
            dma((ny,)),
            dma((nhead,)),
            dma((nz,)),
            dma((nz,)),
            dma((12,)),
        ],
        compiler_params=pltpu.CompilerParams(
            collective_id=0, has_side_effects=True, vmem_limit_bytes=56 << 20
        ),
    )(activations, w_query, w_keyval.T, f_query, f_key, w_out)


def solution(mesh):
    in_specs = (
        P("ctx", None),
        P("ctx", "head"),
        P("ctx", "head"),
        P("head", None, None),
        P(),
        P("ctx", "head"),
    )
    out_specs = P("ctx", "head")
    return jax.shard_map(
        per_device, mesh=mesh, in_specs=in_specs, out_specs=out_specs, check_vma=False
    )
```

```python
import math

import jax
import jax.numpy as jnp
from jax import lax
from jax.experimental import pallas as pl
from jax.experimental.pallas import tpu as pltpu
from jax.sharding import PartitionSpec as P

WINDOW = 64
NX = 4
CORES = 2
MESH = pl.DeviceIdType.MESH
F32 = jnp.float32
BF16 = jnp.bfloat16


def rem(a, b):
    return lax.rem(a, jnp.int32(b))


def div(a, b):
    return lax.div(a, jnp.int32(b))


def features(logits, axis):
    rising = jnp.exp(logits)
    falling = jnp.exp(-logits)
    rising = rising / jnp.sum(rising, axis=axis, keepdims=True)
    falling = falling / jnp.sum(falling, axis=axis, keepdims=True)
    return jnp.concatenate([rising, falling], axis=axis).astype(BF16)


def remote(src, dst, send_sem, recv_sem, ctx, head):
    return pltpu.make_async_remote_copy(
        src_ref=src,
        dst_ref=dst,
        send_sem=send_sem,
        recv_sem=recv_sem,
        device_id={"ctx": ctx, "head": head},
        device_id_type=MESH,
    )


class Spread:
    def __init__(self, size, place, block, device, send_sem, recv_sem):
        self.size, self.place = size, place
        self.block, self.device = block, device
        self.send_sem, self.recv_sem = send_sem, recv_sem

    def at(self, offset):
        return rem(self.place + offset + self.size, self.size)

    def copy(self, source, offset):
        part = self.block(source)
        return remote(
            part,
            part,
            self.send_sem,
            self.recv_sem(source),
            *self.device(self.at(offset)),
        )

    def start(self):
        for offset in (1, -1, 2, -2):
            self.copy(self.place, offset).start()

    def wait(self, offset):
        self.copy(self.at(offset), 1).wait_recv()

    def forward_up(self):
        self.copy(self.at(-2), 1).start()
        self.copy(self.at(-2), 2).start()

    def forward_down(self):
        self.copy(self.at(2), -1).start()

    def near(self):
        self.wait(-2)
        self.forward_up()
        self.wait(2)
        self.forward_down()
        self.wait(-1)
        self.wait(1)

    def far(self):
        for offset in (-3, 3, -4):
            self.wait(offset)


class Ring:
    def __init__(self, size, place, block, device, send_sem, recv_sem, last):
        self.size, self.place = size, place
        self.block, self.device = block, device
        self.send_sem, self.recv_sem, self.last = send_sem, recv_sem, last

    def at(self, offset):
        return rem(self.place + offset + self.size, self.size)

    def copy(self, source, way):
        part = self.block(source)
        return remote(
            part,
            part,
            self.send_sem,
            self.recv_sem(source),
            *self.device(self.at(way)),
        )

    def ways(self, k):
        return (1, -1) if k < self.size // 2 - 1 else (self.last,)

    def start(self):
        for way in self.ways(0):
            self.copy(self.place, way).start()

    def hop(self, k):
        onward = self.ways(k + 1) if k + 1 < self.size // 2 else ()
        for way in self.ways(k):
            source = self.at(-way * (k + 1))
            self.copy(source, way).wait_recv()
            if way in onward:
                self.copy(source, way).start()


class Gather:
    def __init__(self, a, b, y, x, ny, h, send, ax, ay, by, bx):
        self.buf_a, self.buf_b = a, b
        self.y, self.x, self.ny, self.h = y, x, ny, h
        self.send, self.ax, self.bx = send, ax, bx

        def device(place):
            return NX * place + x, h

        def column(j):
            col = rem(x + j, NX)
            return Ring(
                ny,
                y,
                lambda source: a.at[NX * source + col],
                device,
                send.at[0],
                lambda source: ay.at[col, source],
                1 if j < NX // 2 else -1,
            )

        self.columns = [column(j) for j in range(NX)]
        self.b = Spread(
            ny,
            y,
            lambda source: b.at[NX * source + x],
            device,
            send.at[1],
            lambda source: by.at[source],
        )

    def row(self, offset):
        return rem(self.y + offset + self.ny, self.ny)

    def a_copy_x(self, source, to):
        part = self.buf_a.at[NX * self.y + source]
        return remote(
            part, part, self.send.at[0], self.ax.at[source], NX * self.y + to, self.h
        )

    def b_copy_x(self, row, source, to):
        part = self.buf_b.at[NX * row + source]
        return remote(
            part, part, self.send.at[1], self.bx.at[row, source], NX * self.y + to, self.h
        )

    def start(self):
        for j in range(1, NX):
            self.a_copy_x(self.x, rem(self.x + j, NX)).start()
        self.columns[0].start()
        self.b.start()
        self.b_along_x(0)

    def a_row(self):
        for j in (1, 3, 2):
            self.a_copy_x(rem(self.x + j, NX), self.x).wait_recv()
            self.columns[j].start()

    def b_along_x(self, offset):
        row = self.row(offset)
        for way in (1, NX - 1):
            self.b_copy_x(row, self.x, rem(self.x + way, NX)).start()

    def b_relay(self, *offsets):
        for offset in offsets:
            row, way = self.row(offset), 1 if offset % 2 == 0 else NX - 1
            source = rem(self.x + NX - way, NX)
            copy = self.b_copy_x(row, source, rem(self.x + way, NX))
            copy.wait_recv()
            copy.start()

    def b_near(self):
        self.b.near()
        for offset in (-1, 1, -2, 2):
            self.b_along_x(offset)

    def b_far(self):
        for offset in (-3, 3, -4):
            self.b.wait(offset)
            self.b_along_x(offset)

    def a_hop(self, k):
        for j in (1, 3, 2):
            self.columns[j].hop(k)

    def b_wait_x(self, offset):
        row, way = self.row(offset), 1 if offset % 2 == 0 else NX - 1
        for source in (rem(self.x + way, NX), rem(self.x + 2, NX)):
            self.b_copy_x(row, source, self.x).wait_recv()

    def finish(self, sent):
        count = NX * self.ny - 1
        sent(self.buf_a.at[pl.ds(0, count)], self.send.at[0])
        sent(self.buf_b.at[pl.ds(0, count)], self.send.at[1])


def sublayer_kernel(
    nctx,
    nhead,
    x_hbm,
    wq_hbm,
    wkv_ref,
    fq_ref,
    fk_ref,
    wo_hbm,
    out_ref,
    xbuf,
    wq_a,
    wq_b,
    wkv_a,
    wkv_b,
    acc,
    wo_a,
    wo_b,
    kvall,
    bord,
    kfbuf,
    stx,
    sty,
    mz,
    attn,
    xsem,
    lsem,
    q_send,
    q_ax,
    q_ay,
    q_by,
    q_bx,
    o_send,
    o_ax,
    o_ay,
    o_by,
    o_bx,
    wa_x,
    wa_y,
    wb_y,
    wb_x,
    kv_recv,
    b_recv,
    x_recv,
    y_recv,
    m_recv,
    z_recv,
    s_recv,
    misc_send,
):
    ny, nz = nctx // NX, nhead // CORES
    c = lax.axis_index("ctx")
    h = lax.axis_index("head")
    y, x = div(c, NX), rem(c, NX)
    z, core = div(h, CORES), rem(h, CORES)
    tokens = x_hbm.shape[0]
    rows = wq_hbm.shape[0]
    half = rows // 2
    low, olow = wq_a.shape[1], wo_a.shape[2]
    dim = fk_ref.shape[0]
    sibling = CORES * z + 1 - core
    following, previous = rem(c + 1, nctx), rem(c + nctx - 1, nctx)

    barrier = pltpu.get_barrier_semaphore()

    def greet(ctx, head):
        pl.semaphore_signal(
            barrier, inc=1, device_id={"ctx": ctx, "head": head}, device_id_type=MESH
        )

    for j in range(1, NX):
        greet(NX * y + rem(x + j, NX), h)

    @pl.loop(1, ny)
    def _(j):
        greet(NX * rem(y + j, ny) + x, h)

    @pl.loop(1, nhead)
    def _(j):
        greet(c, rem(h + j, nhead))

    greet(following, h)
    greet(previous, h)

    own_q = [
        pltpu.make_async_copy(wq_hbm.at[pl.ds(0, low)], wq_a.at[c], lsem.at[0]),
        pltpu.make_async_copy(
            wq_hbm.at[pl.ds(low, rows - low)], wq_b.at[c], lsem.at[1]
        ),
    ]
    own_o = [
        pltpu.make_async_copy(wo_hbm.at[:, pl.ds(0, olow)], wo_a.at[c], lsem.at[2]),
        pltpu.make_async_copy(
            wo_hbm.at[:, pl.ds(olow, wo_hbm.shape[1] - olow)], wo_b.at[c], lsem.at[3]
        ),
    ]
    for copy in own_q:
        copy.start()

    @pl.loop(0, nctx)
    def _(j):
        pltpu.make_async_copy(
            x_hbm.at[:, pl.ds(pl.multiple_of(j * rows, rows), rows)], xbuf.at[j], xsem
        ).start()

    for copy in own_o:
        copy.start()
    wkv_a[y, x] = wkv_ref[:, :half]
    wkv_b[x, y] = wkv_ref[:, half:]

    pl.semaphore_wait(barrier, (NX - 1) + (ny - 1) + (nhead - 1) + 2)

    q = Gather(wq_a, wq_b, y, x, ny, h, q_send, q_ax, q_ay, q_by, q_bx)
    o = Gather(wo_a, wo_b, y, x, ny, h, o_send, o_ax, o_ay, o_by, o_bx)

    def wa_along_x(source, to):
        part = wkv_a.at[y, source]
        return remote(part, part, misc_send.at[8], wa_x.at[source], NX * y + to, h)

    def wa_over_y(source, to):
        part = wkv_a.at[source]
        return remote(part, part, misc_send.at[9], wa_y.at[source], NX * to + x, h)

    def wb_over_y(source, to):
        part = wkv_b.at[x, source]
        return remote(part, part, misc_send.at[10], wb_y.at[source], NX * to + x, h)

    def wb_along_x(source, to):
        part = wkv_b.at[source]
        return remote(part, part, misc_send.at[11], wb_x.at[source], NX * y + to, h)

    def others(place, size, visit):
        for j in range(1, size):
            visit(rem(place + j, size))

    others(x, NX, lambda to: wa_along_x(x, to).start())
    others(y, ny, lambda to: wb_over_y(y, to).start())
    others(x, NX, lambda source: wa_along_x(source, x).wait_recv())
    others(y, ny, lambda to: wa_over_y(y, to).start())
    others(y, ny, lambda source: wb_over_y(source, y).wait_recv())
    others(x, NX, lambda to: wb_along_x(x, to).start())
    for copy in own_q:
        copy.wait()
    q.start()
    pltpu.make_async_copy(xbuf, xbuf, xsem).wait()
    others(y, ny, lambda source: wa_over_y(source, y).wait_recv())
    others(x, NX, lambda source: wb_along_x(source, x).wait_recv())

    def a_product(offset):
        first = NX * q.row(offset)
        part = jnp.concatenate(
            [xbuf[first + col, :, :low] for col in range(NX)], axis=1
        )
        weights = wq_a[pl.ds(first, NX)].reshape(NX * low, dim)
        return jnp.dot(part, weights, preferred_element_type=F32)

    def b_product(offset):
        first = NX * q.row(offset)
        total = None
        for col in range(NX):
            term = jnp.dot(
                xbuf[first + col, :, low:],
                wq_b[first + col],
                preferred_element_type=F32,
            )
            total = term if total is None else total + term
        return total

    contract_last = (((1,), (1,)), ((), ()))

    def kv_step(block, total):
        row, col = div(block, NX), rem(block, NX)
        return (
            total
            + lax.dot_general(
                wkv_a[row, col],
                xbuf[block, :, :half],
                contract_last,
                preferred_element_type=F32,
            )
            + lax.dot_general(
                wkv_b[col, row],
                xbuf[block, :, half:],
                contract_last,
                preferred_element_type=F32,
            )
        )

    own_kv = lax.fori_loop(
        0, nctx, kv_step, jnp.zeros((wkv_ref.shape[0], tokens), F32), unroll=4
    )
    kvall[h] = own_kv.astype(BF16)

    def to_heads(buffer, sems, send):
        @pl.loop(1, nhead)
        def _(j):
            remote(
                buffer.at[h], buffer.at[h], send, sems.at[h], c, rem(h + j, nhead)
            ).start()

    def from_heads(buffer, sems, send):
        @pl.loop(1, nhead)
        def _(j):
            source = rem(h + j, nhead)
            remote(
                buffer.at[source], buffer.at[source], send, sems.at[source], c, source
            ).wait_recv()

    to_heads(kvall, kv_recv, misc_send.at[0])
    q.a_row()
    q.columns[0].hop(0)
    q.b_relay(0)
    q.b_near()

    from_heads(kvall, kv_recv, misc_send.at[0])
    border = remote(
        kvall.at[:, :, pl.ds(tokens - 2 * WINDOW, 2 * WINDOW)],
        bord,
        misc_send.at[1],
        b_recv,
        following,
        h,
    )
    border.start()
    own = kvall[...].reshape(2 * dim, tokens)
    fk_t = fk_ref[...].astype(F32).T.astype(BF16)
    own_feats = features(jnp.dot(fk_t, own[:dim], preferred_element_type=F32), 0)
    part = 2 * dim // nhead
    edge = 2 * WINDOW
    kfbuf[:, :, edge:] = own_feats.reshape(nhead, part, tokens)

    def state(feats, values):
        matrix = lax.dot_general(
            feats, values, contract_last, preferred_element_type=F32
        )
        total = jnp.sum(feats.astype(F32), axis=1, keepdims=True)
        return matrix, jnp.broadcast_to(total, (part, dim))

    matrix, total = state(kfbuf[h, :, edge:], own[dim:])
    stx[x, 0] = matrix
    stx[x, 1] = total
    for j in range(1, NX):
        remote(
            stx.at[x],
            stx.at[x],
            misc_send.at[2],
            x_recv.at[x],
            NX * y + rem(x + j, NX),
            h,
        ).start()

    q.b_relay(-1, 1, -2, 2)
    q.columns[0].hop(1)
    q.b_far()
    q.a_hop(0)
    acc[...] = a_product(0)

    for j in range(1, NX):
        source = rem(x + j, NX)
        remote(
            stx.at[source],
            stx.at[source],
            misc_send.at[2],
            x_recv.at[source],
            NX * y + source,
            h,
        ).wait_recv()
    row = stx[0] + stx[1] + stx[2] + stx[3]
    before = jnp.zeros_like(row)
    for j in range(NX - 1):
        before = before + stx[j] * jnp.where(j < x, 1.0, 0.0)
    sty[y] = row

    @pl.loop(1, ny)
    def _(j):
        remote(
            sty.at[y],
            sty.at[y],
            misc_send.at[3],
            y_recv.at[y],
            NX * rem(y + j, ny) + x,
            h,
        ).start()

    q.b_relay(-3, 3, -4)
    q.columns[0].hop(2)
    q.a_hop(1)
    for copy in own_o:
        copy.wait()
    o.start()
    for offset in (-1, 1):
        acc[...] += a_product(offset)
    for offset in (0, -1, 1):
        q.b_wait_x(offset)
        acc[...] += b_product(offset)
    q.columns[0].hop(3)

    border.wait_recv()
    edge_kv = bord[...].reshape(2 * dim, edge)
    edge_feats = features(jnp.dot(fk_t, edge_kv[:dim], preferred_element_type=F32), 0)
    kfbuf[:, :, :edge] = edge_feats.reshape(nhead, part, edge)
    lowest = jnp.where(c > 0, WINDOW, edge)
    mine = kfbuf[h, :, :edge].astype(F32)
    held = lax.broadcasted_iota(jnp.int32, mine.shape, 1) >= lowest
    matrix, total = state(jnp.where(held, mine, 0.0).astype(BF16), edge_kv[dim:])

    @pl.loop(1, ny)
    def _(j):
        source = rem(y + j, ny)
        remote(
            sty.at[source],
            sty.at[source],
            misc_send.at[3],
            y_recv.at[source],
            NX * source + x,
            h,
        ).wait_recv()

    for j in range(ny - 1):
        before = before + sty[j] * jnp.where(j < y, 1.0, 0.0)
    mz[h, 0] = (before[0] - matrix).astype(BF16)
    mz[h, 1] = (before[1] - total).astype(BF16)
    to_heads(mz, m_recv, misc_send.at[4])

    q.a_hop(2)
    for offset in (-2, 2):
        acc[...] += a_product(offset)
        q.b_wait_x(offset)
        acc[...] += b_product(offset)
    o.a_row()
    o.columns[0].hop(0)
    o.b_relay(0)
    o.b_near()
    for offset in (-3, 3, -4):
        q.b_wait_x(offset)
        acc[...] += b_product(offset)
    q.a_hop(3)
    for offset in (-3, 3, -4):
        acc[...] += a_product(offset)
    queries = acc[...].astype(BF16)
    query_feats = features(jnp.dot(queries, fq_ref[0], preferred_element_type=F32), 1)

    both = jnp.concatenate([bord[...], kvall[...]], axis=2)
    extent = tokens + edge
    both = both.reshape(2 * dim, extent)
    keys, values = both[:dim], both[dim:]
    key_feats = kfbuf[...].reshape(2 * dim, extent)
    token = lax.broadcasted_iota(jnp.int32, (tokens, extent), 0)
    key_at = lax.broadcasted_iota(jnp.int32, (tokens, extent), 1)
    offset = token + edge - key_at
    held = key_at >= lowest
    inside = (offset >= 0) & (offset < WINDOW) & held
    beyond = (offset >= WINDOW) & held
    scores = jnp.dot(queries, keys, preferred_element_type=F32) * (1.0 / math.sqrt(dim))
    far = jnp.dot(query_feats, key_feats, preferred_element_type=F32)
    weights = jnp.where(inside, jnp.exp(scores), 0.0) + jnp.where(beyond, far, 0.0)
    numerator = lax.dot_general(
        weights.astype(BF16), values, contract_last, preferred_element_type=F32
    )
    denominator = jnp.sum(weights, axis=1, keepdims=True)

    from_heads(mz, m_recv, misc_send.at[4])
    matrix = mz[:, 0].reshape(2 * dim, dim)
    totals = mz[:, 1].reshape(2 * dim, dim)
    numerator = numerator + jnp.dot(query_feats, matrix, preferred_element_type=F32)
    denominator = denominator + jnp.dot(query_feats, totals, preferred_element_type=F32)
    attn[z, core] = (numerator / denominator).astype(BF16)

    a = Spread(
        nz,
        z,
        lambda source: attn.at[source, core],
        lambda place: (c, CORES * place + core),
        misc_send.at[5],
        lambda source: z_recv.at[source],
    )

    def sibling_copy(block, side):
        part = attn.at[block, side]
        return remote(part, part, misc_send.at[6], s_recv.at[block], c, sibling)

    a.start()
    sibling_copy(z, core).start()
    o.a_hop(0)
    o.columns[0].hop(1)
    o.b_relay(-1, 1, -2, 2)
    o.b_far()
    a.wait(-2)
    a.forward_up()
    sibling_copy(a.at(-2), core).start()
    a.wait(2)
    a.forward_down()
    sibling_copy(a.at(2), core).start()
    o.a_hop(1)
    o.columns[0].hop(2)
    o.b_relay(-3, 3, -4)
    for offset in (-1, 1, -3, 3, -4):
        a.wait(offset)
        sibling_copy(a.at(offset), core).start()
    o.a_hop(2)
    o.columns[0].hop(3)
    for offset in range(ny):
        o.b_wait_x(offset)
    for offset in range(nz):
        sibling_copy(a.at(offset), 1 - core).wait_recv()

    heads = jnp.concatenate([attn[j // CORES, j % CORES] for j in range(nhead)], axis=1)
    for weights, start in ((wo_b, olow), (wo_a, 0)):
        if start == 0:
            o.a_hop(3)
        for at in range(0, weights.shape[2], 2 * dim):
            size = min(2 * dim, weights.shape[2] - at)
            tile = weights[:, :, at : at + size].reshape(nhead * dim, size)
            out_ref[:, start : start + size] = jnp.dot(
                heads, tile, preferred_element_type=F32
            ).astype(BF16)
            start += size

    def sent(ref, sem):
        remote(ref, ref, sem, b_recv, following, h).wait_send()

    q.finish(sent)
    o.finish(sent)
    sent(kvall.at[pl.ds(0, nhead - 1)], misc_send.at[0])
    sent(bord, misc_send.at[1])
    sent(stx.at[pl.ds(0, NX - 1)], misc_send.at[2])
    sent(sty.at[pl.ds(0, ny - 1)], misc_send.at[3])
    sent(mz.at[pl.ds(0, nhead - 1)], misc_send.at[4])
    sent(attn.at[pl.ds(0, nz - 1), 0], misc_send.at[5])
    sent(attn.at[:, 0], misc_send.at[6])
    sent(wkv_a.at[0, pl.ds(0, NX - 1)], misc_send.at[8])
    sent(wkv_a.at[pl.ds(0, ny - 1)], misc_send.at[9])
    sent(wkv_b.at[0, pl.ds(0, ny - 1)], misc_send.at[10])
    sent(wkv_b.at[pl.ds(0, NX - 1)], misc_send.at[11])


def per_device(activations, w_query, w_keyval, f_query, f_key, w_out):
    nctx, nhead = lax.axis_size("ctx"), lax.axis_size("head")
    ny, nz = nctx // NX, nhead // CORES
    tokens = activations.shape[0]
    rows, width = w_keyval.shape
    low, orows = rows // 2, w_out.shape[0]
    dim, columns = f_key.shape[0], w_out.shape[1]
    olow = 3 * columns // 8
    extent = tokens + 2 * WINDOW
    part = 2 * dim // nhead

    def kernel(*refs):
        sublayer_kernel(nctx, nhead, *refs)

    dma = pltpu.SemaphoreType.DMA
    gather_sems = [
        dma((2,)),
        dma((NX,)),
        dma((NX, ny)),
        dma((ny,)),
        dma((ny, NX)),
    ]
    anywhere = pl.BlockSpec(memory_space=pl.ANY)
    vmem = pl.BlockSpec(memory_space=pltpu.VMEM)
    return pl.pallas_call(
        kernel,
        out_shape=jax.ShapeDtypeStruct((tokens, columns), BF16),
        in_specs=[anywhere, anywhere, vmem, vmem, vmem, anywhere],
        out_specs=vmem,
        scratch_shapes=[
            pltpu.VMEM((nctx, tokens, rows), BF16),
            pltpu.VMEM((nctx, low, dim), BF16),
            pltpu.VMEM((nctx, rows - low, dim), BF16),
            pltpu.VMEM((ny, NX, width, rows // 2), BF16),
            pltpu.VMEM((NX, ny, width, rows // 2), BF16),
            pltpu.VMEM((tokens, dim), F32),
            pltpu.VMEM((nctx, orows, olow), BF16),
            pltpu.VMEM((nctx, orows, columns - olow), BF16),
            pltpu.VMEM((nhead, width, tokens), BF16),
            pltpu.VMEM((nhead, width, 2 * WINDOW), BF16),
            pltpu.VMEM((nhead, part, extent), BF16),
            pltpu.VMEM((NX, 2, part, dim), F32),
            pltpu.VMEM((ny, 2, part, dim), F32),
            pltpu.VMEM((nhead, 2, part, dim), BF16),
            pltpu.VMEM((nz, CORES, tokens, dim), BF16),
            dma,
            dma((4,)),
            *gather_sems,
            *gather_sems,
            dma((NX,)),
            dma((ny,)),
            dma((ny,)),
            dma((NX,)),
            dma((nhead,)),
            dma,
            dma((NX,)),
            dma((ny,)),
            dma((nhead,)),
            dma((nz,)),
            dma((nz,)),
            dma((12,)),
        ],
        compiler_params=pltpu.CompilerParams(
            collective_id=0, has_side_effects=True, vmem_limit_bytes=56 << 20
        ),
    )(activations, w_query, w_keyval.T, f_query, f_key, w_out)


def solution(mesh):
    in_specs = (
        P("ctx", None),
        P("ctx", "head"),
        P("ctx", "head"),
        P("head", None, None),
        P(),
        P("ctx", "head"),
    )
    out_specs = P("ctx", "head")
    return jax.shard_map(
        per_device, mesh=mesh, in_specs=in_specs, out_specs=out_specs, check_vma=False
    )
```
